256 devices in a mesh: alpha: 16 (over y, x_hi, core), beta: 16 (over x_lo, z).
Axes of the slice: x: 4 (x_hi: 2, x_lo: 2; x = x_hi * 2 + x_lo), y: 4, z: 8, core: 2. Of those that a mesh axis runs over, the one named last changes fastest.
Arguments:
- coefficients: float32 [12288, 12288], P('alpha', 'beta'), may hold values from -6 to 6
- beta_blocks: float32 [32, 3, 384, 384], P('beta'), may hold values from -0.1875 to 0.1875
- alpha_blocks: float32 [32, 3, 384, 384], P('alpha'), may hold values from -0.1875 to 0.1875
- beta_links: int32 [32, 3], P('beta'), may hold values from 0 to 31, as said below
- alpha_links: int32 [32, 3], P('alpha'), may hold values from 0 to 31, as said below
- beta_count: int32 [32], P('beta'), may hold values from 1 to 3, as said below
- alpha_count: int32 [32], P('alpha'), may hold values from 1 to 3, as said below
Outputs:
- sigma_slab: float32 [12288, 12288], P('alpha', 'beta')
The draws below stay inside these ranges and needn't reach their ends.
Inputs may be any that keep to these rules, and one draw needn't show every extreme that they name: `beta_links`: each row lists 3 distinct beta groups whose cyclic distance from the row's own group is at most 2. `alpha_links`: each row lists 3 distinct alpha groups whose cyclic distance from the row's own group is at most 2. `beta_count`: some group uses all 3 couplings. `alpha_count`: some group uses all 3 couplings.
All inputs are finite; a program needn't handle non-finite values.
Results may differ from the reference program's by a relative error of at most 0.0003.
Values sent between devices are 32-bit elements; how exact they have to be, the bound alone decides.
A program may use at most 128 MiB of HBM per device.

```python
import jax
import jax.numpy as jnp
from jax import lax

G = 384
REACH = 2
LIST = 3
GROUPS_A = 32
GROUPS_B = 32
SA = 12288
SB = 12288


def link_table(key, groups):
    row_keys = jax.random.split(key, groups)
    orders = jax.vmap(lambda one_key: jax.random.permutation(one_key, 2 * REACH + 1))(row_keys)
    offsets = orders[:, :LIST] - REACH
    return ((jnp.arange(groups)[:, None] + offsets) % groups).astype(jnp.int32)


def count_table(key, groups):
    counts = jax.random.randint(key, (groups,), 1, LIST + 1)
    position = jax.random.randint(jax.random.fold_in(key, 5), (), 0, groups)
    return counts.at[position].set(LIST).astype(jnp.int32)


def draw_beta_links(key, part):
    return link_table(jax.random.fold_in(key, 11), GROUPS_B)


def draw_alpha_links(key, part):
    return link_table(jax.random.fold_in(key, 12), GROUPS_A)


def draw_beta_count(key, part):
    return count_table(jax.random.fold_in(key, 13), GROUPS_B)


def draw_alpha_count(key, part):
    return count_table(jax.random.fold_in(key, 14), GROUPS_A)


def shard_levels(stream_key, dims, cuts, least, largest):
    loudness, own = 1.0, jax.random.fold_in(stream_key, 6)
    for axis_at, parts in cuts:
        draws = jnp.exp(jax.random.uniform(jax.random.fold_in(own, axis_at), (parts,), jnp.float32, least / len(cuts), largest / len(cuts)))
        loudness = loudness * jnp.repeat(draws, dims[axis_at] // parts).reshape([-1 if axis == axis_at else 1 for axis in range(len(dims))])
    return loudness


def bell_draw(own_key, shape, width, reach, cuts=(), held_as=jnp.bfloat16):
    values = jax.random.normal(own_key, shape, jnp.float32) * width
    if len(cuts) > 0:
        values = shard_levels(own_key, shape, cuts, -0.22, 0.18) * values
    return jnp.clip(values, min=-reach, max=reach).astype(held_as)


def setup_inputs(seed: int = 0) -> dict:
    keys = jax.random.split(jax.random.key(seed), 8)
    return {
        "coefficients": bell_draw(keys[0], (SA, SB), 1.0, 6.0, ((0, 16), (1, 16)), jnp.float32),
        "beta_blocks": bell_draw(keys[1], (GROUPS_B, LIST, G, G), (G * LIST) ** -0.5, 0.1875, ((0, 16),), jnp.float32),
        "alpha_blocks": bell_draw(keys[2], (GROUPS_A, LIST, G, G), (G * LIST) ** -0.5, 0.1875, ((0, 16),), jnp.float32),
        "beta_links": draw_beta_links(jax.random.fold_in(keys[7], 71), 0),
        "alpha_links": draw_alpha_links(jax.random.fold_in(keys[7], 71), 0),
        "beta_count": draw_beta_count(jax.random.fold_in(keys[7], 71), 0),
        "alpha_count": draw_alpha_count(jax.random.fold_in(keys[7], 71), 0),
    }


def beta_part_of(coefficients, beta_blocks, beta_links, beta_count):
    def one_group(group):
        def accumulate(position, running):
            source = beta_links[group, position].astype(jnp.int32)
            columns = lax.dynamic_slice_in_dim(coefficients, (source * G).astype(jnp.int32), G, 1)
            return running + jnp.dot(columns, beta_blocks[group, position], precision=lax.Precision.HIGHEST, preferred_element_type=jnp.float32)
        start = jnp.zeros((coefficients.shape[0], G), coefficients.dtype)
        return lax.fori_loop(0, beta_count[group], accumulate, start)
    pieces = lax.map(one_group, jnp.arange(GROUPS_B, dtype=jnp.int32))
    return jnp.transpose(pieces, (1, 0, 2)).reshape(coefficients.shape[0], GROUPS_B * G)


def alpha_part_of(coefficients, alpha_blocks, alpha_links, alpha_count):
    def one_group(group):
        def accumulate(position, running):
            source = alpha_links[group, position].astype(jnp.int32)
            rows = lax.dynamic_slice_in_dim(coefficients, (source * G).astype(jnp.int32), G, 0)
            return running + jnp.dot(alpha_blocks[group, position], rows, precision=lax.Precision.HIGHEST, preferred_element_type=jnp.float32)
        start = jnp.zeros((G, coefficients.shape[1]), coefficients.dtype)
        return lax.fori_loop(0, alpha_count[group], accumulate, start)
    pieces = lax.map(one_group, jnp.arange(GROUPS_A, dtype=jnp.int32))
    return pieces.reshape(GROUPS_A * G, coefficients.shape[1])


def reference(coefficients, beta_blocks, alpha_blocks, beta_links, alpha_links, beta_count, alpha_count):
    beta_part = beta_part_of(coefficients, beta_blocks, beta_links, beta_count)
    alpha_part = alpha_part_of(coefficients, alpha_blocks, alpha_links, alpha_count)
    return beta_part + alpha_part
```

```python
import functools

import jax
import jax.numpy as jnp
from jax import lax
from jax.experimental import pallas as pl
from jax.experimental.pallas import tpu as pltpu
from jax.sharding import PartitionSpec as P

MESH = pl.DeviceIdType.MESH
G = 384
GPD = 2
LIST = 3
S = G * GPD
CHUNKS = 24
R = S // CHUNKS


def split(x):
    high = x.astype(jnp.bfloat16)
    return high, (x - high.astype(jnp.float32)).astype(jnp.bfloat16)


def product(a_high, a_low, b_high, b_low):
    dot = functools.partial(jnp.dot, preferred_element_type=jnp.float32)
    return dot(a_high, b_high) + dot(a_low, b_high) + dot(a_high, b_low)


def kernel(
    na, nb,
    c_ref, hb_ref, ha_ref, lb_ref, la_ref, cb_ref, ca_ref,
    out_ref,
    own, near, far, left, right, relay, hb, ha,
    own_h, own_l, near_h, near_l, kb_h, kb_l, ka_h, ka_l,
    send_sem, recv_sem, near_send, near_recv, local_sem,
):
    a, b = lax.axis_index("alpha"), lax.axis_index("beta")
    nz = nb // 2
    core, z = lax.rem(a, 2), lax.rem(b, nz)
    column = b - z
    core_device = (a + 1 - 2 * core, b)
    inner_device = (a, lax.rem(b + nz, nb))
    outer_device = (lax.rem(a + 2 * core + na - 1, na), lax.rem(b + nz, nb))
    up_device = (a, column + lax.rem(z + 1, nz))
    down_device = (a, column + lax.rem(z + nz - 1, nz))

    own_copy = pltpu.make_async_copy(c_ref, own, local_sem.at[0])
    hb_copy = pltpu.make_async_copy(hb_ref, hb, local_sem.at[1])
    ha_copy = pltpu.make_async_copy(ha_ref, ha, local_sem.at[2])
    own_copy.start()
    hb_copy.start()
    ha_copy.start()

    barrier = pltpu.get_barrier_semaphore()
    for device in (core_device, inner_device, outer_device, up_device, down_device):
        pl.semaphore_signal(barrier, inc=1, device_id=device, device_id_type=MESH)
    pl.semaphore_wait(barrier, 5)

    def remote(source, target, flow, k, device):
        rows = pl.ds(k * R, R)
        return pltpu.make_async_remote_copy(
            src_ref=source.at[rows],
            dst_ref=target.at[rows],
            send_sem=send_sem.at[flow, k],
            recv_sem=recv_sem.at[flow, k],
            device_id=device,
            device_id_type=MESH,
        )

    def to_inner(k):
        return remote(c_ref, relay, 0, k, inner_device)

    def to_outer(k):
        return remote(relay, far, 1, k, outer_device)

    def to_up(k, source=c_ref):
        return remote(source, left, 2, k, up_device)

    def to_down(k, source=c_ref):
        return remote(source, right, 3, k, down_device)

    to_core = pltpu.make_async_remote_copy(
        src_ref=c_ref, dst_ref=near, send_sem=near_send, recv_sem=near_recv,
        device_id=core_device, device_id_type=MESH,
    )

    @pl.loop(0, CHUNKS)
    def _(k):
        to_inner(k).start()

        @pl.when(z != nz - 1)
        def _():
            to_up(k).start()

        @pl.when(z != 0)
        def _():
            to_down(k).start()

    to_core.start()

    def forward(k):
        to_inner(k).wait_recv()
        to_outer(k).start()

        @pl.when(z == nz - 1)
        def _():
            to_up(k, relay).start()

        @pl.when(z == 0)
        def _():
            to_down(k, relay).start()

    def select(blocks, links, counts, t, group, rows):
        total = None
        for l in range(LIST):
            used = jnp.logical_and(links[t, l] == group, l < counts[t])
            term = jnp.where(used, 1.0, 0.0) * blocks[t, l, rows, :]
            total = term if total is None else total + term
        return total

    def build(s):
        for t in range(GPD):
            beta_group = lax.rem(GPD * (b + nb - 1) + s, GPD * nb)
            alpha_group = lax.rem(GPD * (a + na - 1) + s, GPD * na)
            at = pl.multiple_of(s * G, 128)

            @pl.loop(0, G // 64)
            def _(i):
                rows = pl.ds(pl.multiple_of(i * 64, 64), 64)
                high, low = split(select(hb, lb_ref, cb_ref, t, beta_group, rows))
                to = (pl.ds(pl.multiple_of(at + i * 64, 64), 64), pl.ds(t * G, G))
                kb_h[to], kb_l[to] = high, low
                high, low = split(select(ha, la_ref, ca_ref, t, alpha_group, rows))
                to = (pl.ds(pl.multiple_of(t * G + i * 64, 64), 64), pl.ds(at, G))
                ka_h[to], ka_l[to] = high, low

        rows = pl.ds(pl.multiple_of(s * 128, 128), 128)
        own_h[rows, :], own_l[rows, :] = split(own[rows, :])

    near_at = jnp.where(core == 1, 0, 2 * S)
    far_at = 2 * S - near_at

    own_copy.wait()
    hb_copy.wait()
    ha_copy.wait()

    @pl.loop(0, 6)
    def _(s):
        forward(s)
        build(s)

    to_core.wait_recv()

    @pl.loop(0, 3)
    def _(i):
        forward(6 + i)
        rows = pl.ds(pl.multiple_of(i * 256, 256), 256)
        mine = pl.ds(S, S)
        near_h[rows, :], near_l[rows, :] = split(near[rows, :])
        out_ref[rows, :] = product(own_h[rows, :], own_l[rows, :], kb_h[mine, :], kb_l[mine, :])
        out_ref[rows, :] += product(ka_h[rows, mine], ka_l[rows, mine], own_h[...], own_l[...])

    @pl.loop(0, 3)
    def _(i):
        forward(9 + i)
        rows = pl.ds(pl.multiple_of(i * 256, 256), 256)
        mine = pl.ds(pl.multiple_of(near_at, 256), S)
        out_ref[rows, :] += product(ka_h[rows, mine], ka_l[rows, mine], near_h[...], near_l[...])

    def sides(j):
        rows = pl.ds(pl.multiple_of(j * 128, 128), 128)

        @pl.loop(4 * j, 4 * j + 4)
        def _(k):
            to_up(k).wait_recv()
            to_down(k).wait_recv()

        for part, at in ((left, 0), (right, 2 * S)):
            mine = pl.ds(at, S)
            out_ref[rows, :] += product(*split(part[rows, :]), kb_h[mine, :], kb_l[mine, :])

    def outer(j):
        rows = pl.ds(pl.multiple_of(j * 128, 128), 128)
        mine = pl.ds(pl.multiple_of(far_at + j * 128, 128), 128)

        @pl.loop(4 * j, 4 * j + 4)
        def _(k):
            to_outer(k).wait_recv()

        high, low = split(far[rows, :])

        @pl.loop(0, 3)
        def _(i):
            block = pl.ds(pl.multiple_of(i * 256, 256), 256)
            out_ref[block, :] += product(ka_h[block, mine], ka_l[block, mine], high, low)

    @pl.loop(0, 4)
    def _(j):
        forward(12 + 2 * j)
        sides(j)
        forward(13 + 2 * j)
        outer(j)

    @pl.loop(20, CHUNKS)
    def _(k):
        forward(k)

    @pl.loop(4, 6)
    def _(j):
        sides(j)
        outer(j)

    to_core.wait_send()

    @pl.loop(0, CHUNKS)
    def _(k):
        to_inner(k).wait_send()
        to_outer(k).wait_send()
        to_up(k).wait_send()
        to_down(k).wait_send()


def solution(mesh):
    na, nb = mesh.shape["alpha"], mesh.shape["beta"]

    def on_device(
        coefficients, beta_blocks, alpha_blocks, beta_links, alpha_links, beta_count, alpha_count
    ):
        block = pltpu.VMEM((S, S), jnp.float32)
        listed = pltpu.VMEM((GPD, LIST, G, G), jnp.float32)
        half = pltpu.VMEM((S, S), jnp.bfloat16)
        tall = pltpu.VMEM((3 * S, S), jnp.bfloat16)
        wide = pltpu.VMEM((S, 3 * S), jnp.bfloat16)
        return pl.pallas_call(
            functools.partial(kernel, na, nb),
            out_shape=jax.ShapeDtypeStruct((S, S), jnp.float32),
            in_specs=[pl.BlockSpec(memory_space=pl.ANY)] * 3
            + [pl.BlockSpec(memory_space=pltpu.SMEM)] * 4,
            out_specs=pl.BlockSpec(memory_space=pltpu.VMEM),
            scratch_shapes=[block] * 6
            + [listed] * 2
            + [half] * 4
            + [tall, tall, wide, wide]
            + [
                pltpu.SemaphoreType.DMA((4, CHUNKS)),
                pltpu.SemaphoreType.DMA((4, CHUNKS)),
                pltpu.SemaphoreType.DMA(()),
                pltpu.SemaphoreType.DMA(()),
                pltpu.SemaphoreType.DMA((3,)),
            ],
            compiler_params=pltpu.CompilerParams(
                collective_id=0, has_side_effects=True, vmem_limit_bytes=58 * 2**20
            ),
            name="sigma",
        )(
            coefficients, beta_blocks, alpha_blocks,
            beta_links, alpha_links, beta_count, alpha_count,
        )

    return jax.shard_map(
        on_device,
        mesh=mesh,
        in_specs=(
            P("alpha", "beta"),
            P("beta", None, None, None),
            P("alpha", None, None, None),
            P("beta", None),
            P("alpha", None),
            P("beta"),
            P("alpha"),
        ),
        out_specs=P("alpha", "beta"),
        check_vma=False,
    )
```

```python
import functools

import jax
import jax.numpy as jnp
from jax import lax
from jax.experimental import pallas as pl
from jax.experimental.pallas import tpu as pltpu
from jax.sharding import PartitionSpec as P

MESH = pl.DeviceIdType.MESH
G = 384
GPD = 2
LIST = 3
S = G * GPD
CHUNKS = 24
R = S // CHUNKS
TAIL = 64


def split(x):
    high = x.astype(jnp.bfloat16)
    return high, (x - high.astype(jnp.float32)).astype(jnp.bfloat16)


def product(a_high, a_low, b_high, b_low):
    dot = functools.partial(jnp.dot, preferred_element_type=jnp.float32)
    return dot(a_high, b_high) + dot(a_low, b_high) + dot(a_high, b_low)


def kernel(
    na, nb,
    c_ref, hb_ref, ha_ref, lb_ref, la_ref, cb_ref, ca_ref,
    out_ref,
    own, near, far, left, right, relay, hb, ha,
    own_h, own_l, near_h, near_l, kb_h, kb_l, ka_h, ka_l, tail,
    send_sem, recv_sem, near_send, near_recv, local_sem,
):
    a, b = lax.axis_index("alpha"), lax.axis_index("beta")
    nz = nb // 2
    core, z = lax.rem(a, 2), lax.rem(b, nz)
    column = b - z
    core_device = (a + 1 - 2 * core, b)
    inner_device = (a, lax.rem(b + nz, nb))
    outer_device = (lax.rem(a + 2 * core + na - 1, na), lax.rem(b + nz, nb))
    up_device = (a, column + lax.rem(z + 1, nz))
    down_device = (a, column + lax.rem(z + nz - 1, nz))

    own_copy = pltpu.make_async_copy(c_ref, own, local_sem.at[0])
    hb_copy = pltpu.make_async_copy(hb_ref, hb, local_sem.at[1])
    ha_copy = pltpu.make_async_copy(ha_ref, ha, local_sem.at[2])
    own_copy.start()
    hb_copy.start()
    ha_copy.start()

    barrier = pltpu.get_barrier_semaphore()
    for device in (core_device, inner_device, outer_device, up_device, down_device):
        pl.semaphore_signal(barrier, inc=1, device_id=device, device_id_type=MESH)
    pl.semaphore_wait(barrier, 5)

    def remote(source, target, flow, k, device):
        rows = pl.ds(k * R, R)
        return pltpu.make_async_remote_copy(
            src_ref=source.at[rows],
            dst_ref=target.at[rows],
            send_sem=send_sem.at[flow, k],
            recv_sem=recv_sem.at[flow, k],
            device_id=device,
            device_id_type=MESH,
        )

    def to_inner(k):
        return remote(c_ref, relay, 0, k, inner_device)

    def to_outer(k):
        return remote(relay, far, 1, k, outer_device)

    def to_up(k, source=c_ref):
        return remote(source, left, 2, k, up_device)

    def to_down(k, source=c_ref):
        return remote(source, right, 3, k, down_device)

    to_core = pltpu.make_async_remote_copy(
        src_ref=c_ref, dst_ref=near, send_sem=near_send, recv_sem=near_recv,
        device_id=core_device, device_id_type=MESH,
    )

    @pl.loop(0, CHUNKS)
    def _(k):
        to_inner(k).start()

        @pl.when(z != nz - 1)
        def _():
            to_up(k).start()

        @pl.when(z != 0)
        def _():
            to_down(k).start()

    to_core.start()

    def forward(k):
        to_inner(k).wait_recv()
        to_outer(k).start()

        @pl.when(z == nz - 1)
        def _():
            to_up(k, relay).start()

        @pl.when(z == 0)
        def _():
            to_down(k, relay).start()

    def select(blocks, links, counts, t, group, rows):
        total = None
        for l in range(LIST):
            used = jnp.logical_and(links[t, l] == group, l < counts[t])
            term = jnp.where(used, 1.0, 0.0) * blocks[t, l, rows, :]
            total = term if total is None else total + term
        return total

    def build(s):
        for t in range(GPD):
            beta_group = lax.rem(GPD * (b + nb - 1) + s, GPD * nb)
            alpha_group = lax.rem(GPD * (a + na - 1) + s, GPD * na)
            at = pl.multiple_of(s * G, 128)

            @pl.loop(0, G // 64)
            def _(i):
                rows = pl.ds(pl.multiple_of(i * 64, 64), 64)
                high, low = split(select(hb, lb_ref, cb_ref, t, beta_group, rows))
                to = (pl.ds(pl.multiple_of(at + i * 64, 64), 64), pl.ds(t * G, G))
                kb_h[to], kb_l[to] = high, low
                high, low = split(select(ha, la_ref, ca_ref, t, alpha_group, rows))
                to = (pl.ds(pl.multiple_of(t * G + i * 64, 64), 64), pl.ds(at, G))
                ka_h[to], ka_l[to] = high, low

        rows = pl.ds(pl.multiple_of(s * 128, 128), 128)
        own_h[rows, :], own_l[rows, :] = split(own[rows, :])

    def arrived(first, size, *copies):
        @pl.loop(first // R, (first + size) // R)
        def _(k):
            for copy in copies:
                copy(k).wait_recv()

    def sides(first, size):
        rows = pl.ds(first, size)
        arrived(first, size, to_up, to_down)
        for block, at in ((left, 0), (right, 2 * S)):
            theirs = pl.ds(at, S)
            out_ref[rows, :] += product(*split(block[rows, :]), kb_h[theirs, :], kb_l[theirs, :])

    def outer(j):
        rows = pl.ds(pl.multiple_of(j * 128, 128), 128)
        theirs = pl.ds(pl.multiple_of(far_at + j * 128, 128), 128)
        arrived(j * 128, 128, to_outer)
        high, low = split(far[rows, :])

        @pl.loop(0, 3)
        def _(i):
            block = pl.ds(pl.multiple_of(i * 256, 256), 256)
            out_ref[block, :] += product(ka_h[block, theirs], ka_l[block, theirs], high, low)

    def pack_tail(i):
        theirs = pl.ds(pl.multiple_of(far_at + S - 2 * TAIL, 128), 2 * TAIL)

        @pl.loop(0, 4)
        def _(step):
            rows = pl.ds(pl.multiple_of(i * 256 + step * 64, 64), 64)
            high = ka_h[rows, theirs].astype(jnp.float32)
            low = ka_l[rows, theirs].astype(jnp.float32)
            other_high, other_low = pltpu.roll(high, TAIL, 1), pltpu.roll(low, TAIL, 1)
            first = lax.broadcasted_iota(jnp.int32, high.shape, 1) < TAIL
            for part, left_half, right_half in ((0, high, other_low), (1, other_high, low)):
                tail[part, rows, : 2 * TAIL] = jnp.where(first, left_half, right_half).astype(jnp.bfloat16)
                tail[part, rows, 2 * TAIL :] = jnp.where(first, left_half, 0.0).astype(jnp.bfloat16)

    def outer_tail(part):
        first = S - TAIL * (2 - part)
        arrived(first, TAIL, to_outer)
        high, low = split(far[pl.ds(first, TAIL), :])
        stacked = jnp.concatenate([high, high, low, jnp.zeros_like(low)], axis=0)

        @pl.loop(0, 3)
        def _(i):
            block = pl.ds(pl.multiple_of(i * 256, 256), 256)
            out_ref[block, :] += jnp.dot(
                tail[part, block, :], stacked, preferred_element_type=jnp.float32
            )

    near_at = jnp.where(core == 1, 0, 2 * S)
    far_at = 2 * S - near_at

    own_copy.wait()
    hb_copy.wait()
    ha_copy.wait()

    @pl.loop(0, 6)
    def _(s):
        forward(s)
        build(s)

    to_core.wait_recv()
    mine = pl.ds(S, S)

    @pl.loop(0, 3)
    def _(i):
        forward(6 + i)
        rows = pl.ds(pl.multiple_of(i * 256, 256), 256)
        out_ref[rows, :] = product(own_h[rows, :], own_l[rows, :], kb_h[mine, :], kb_l[mine, :])

    @pl.loop(0, 3)
    def _(i):
        forward(9 + i)
        rows = pl.ds(pl.multiple_of(i * 256, 256), 256)
        near_h[rows, :], near_l[rows, :] = split(near[rows, :])
        out_ref[rows, :] += product(ka_h[rows, mine], ka_l[rows, mine], own_h[...], own_l[...])

    @pl.loop(0, 3)
    def _(i):
        forward(12 + i)
        rows = pl.ds(pl.multiple_of(i * 256, 256), 256)
        theirs = pl.ds(pl.multiple_of(near_at, 256), S)
        out_ref[rows, :] += product(ka_h[rows, theirs], ka_l[rows, theirs], near_h[...], near_l[...])
        pack_tail(i)

    @pl.loop(0, 4)
    def _(j):
        forward(15 + 2 * j)
        sides(pl.multiple_of(j * 128, 128), 128)
        forward(16 + 2 * j)
        outer(j)

    forward(CHUNKS - 1)
    sides(512, 128)
    outer(4)
    to_core.wait_send()

    def wait_sends(first, last):
        @pl.loop(first, last)
        def _(k):
            to_inner(k).wait_send()
            to_outer(k).wait_send()
            to_up(k).wait_send()
            to_down(k).wait_send()

    wait_sends(0, CHUNKS - 4)
    for part in range(2):
        sides(S - TAIL * (2 - part), TAIL)
        outer_tail(part)
    wait_sends(CHUNKS - 4, CHUNKS)


def store(total_ref, out_ref, sem):
    copy = pltpu.make_async_copy(total_ref, out_ref, sem)
    copy.start()
    copy.wait()


def solution(mesh):
    na, nb = mesh.shape["alpha"], mesh.shape["beta"]

    def on_device(
        coefficients, beta_blocks, alpha_blocks, beta_links, alpha_links, beta_count, alpha_count
    ):
        block = pltpu.VMEM((S, S), jnp.float32)
        listed = pltpu.VMEM((GPD, LIST, G, G), jnp.float32)
        half = pltpu.VMEM((S, S), jnp.bfloat16)
        tall = pltpu.VMEM((3 * S, S), jnp.bfloat16)
        wide = pltpu.VMEM((S, 3 * S), jnp.bfloat16)
        total = pl.pallas_call(
            functools.partial(kernel, na, nb),
            out_shape=pltpu.VMEM((S, S), jnp.float32),
            in_specs=[pl.BlockSpec(memory_space=pltpu.HBM)] * 3
            + [pl.BlockSpec(memory_space=pltpu.SMEM)] * 4,
            out_specs=pl.BlockSpec(memory_space=pltpu.VMEM),
            scratch_shapes=[block] * 6
            + [listed] * 2
            + [half] * 4
            + [tall, tall, wide, wide, pltpu.VMEM((2, S, 4 * TAIL), jnp.bfloat16)]
            + [
                pltpu.SemaphoreType.DMA((4, CHUNKS)),
                pltpu.SemaphoreType.DMA((4, CHUNKS)),
                pltpu.SemaphoreType.DMA(()),
                pltpu.SemaphoreType.DMA(()),
                pltpu.SemaphoreType.DMA((3,)),
            ],
            compiler_params=pltpu.CompilerParams(
                collective_id=0, has_side_effects=True, vmem_limit_bytes=58 * 2**20
            ),
            name="sigma",
        )(
            coefficients, beta_blocks, alpha_blocks,
            beta_links, alpha_links, beta_count, alpha_count,
        )
        return pl.pallas_call(
            store,
            out_shape=jax.ShapeDtypeStruct((S, S), jnp.float32),
            in_specs=[pl.BlockSpec(memory_space=pltpu.VMEM)],
            out_specs=pl.BlockSpec(memory_space=pl.ANY),
            scratch_shapes=[pltpu.SemaphoreType.DMA],
            compiler_params=pltpu.CompilerParams(vmem_limit_bytes=8 * 2**20),
            name="store",
        )(total)

    return jax.shard_map(
        on_device,
        mesh=mesh,
        in_specs=(
            P("alpha", "beta"),
            P("beta", None, None, None),
            P("alpha", None, None, None),
            P("beta", None),
            P("alpha", None),
            P("beta"),
            P("alpha"),
        ),
        out_specs=P("alpha", "beta"),
        check_vma=False,
    )
```

```python
import functools

import jax
import jax.numpy as jnp
from jax import lax
from jax.experimental import pallas as pl
from jax.experimental.pallas import tpu as pltpu
from jax.sharding import PartitionSpec as P

MESH = pl.DeviceIdType.MESH
G = 384
GPD = 2
LIST = 3
S = G * GPD
R = 64
EVEN = 10
LAST = 96
CHUNKS = EVEN + 2
FINAL = CHUNKS - 1


def split(x):
    high = x.astype(jnp.bfloat16)
    return high, (x - high.astype(jnp.float32)).astype(jnp.bfloat16)


def product(a_high, a_low, b_high, b_low):
    dot = functools.partial(jnp.dot, preferred_element_type=jnp.float32)
    return dot(a_high, b_high) + dot(a_low, b_high) + dot(a_high, b_low)


def chunk(k):
    if isinstance(k, int) and k >= EVEN:
        return pl.ds(*((EVEN * R, S - EVEN * R - LAST), (S - LAST, LAST))[k - EVEN])
    return pl.ds(k * R, R)


def kernel(
    na, nb,
    c_ref, hb_ref, ha_ref, lb_ref, la_ref, cb_ref, ca_ref,
    out_ref,
    own, near, far, left, right, relay, detour, hb, ha,
    own_h, own_l, near_h, near_l, kb_h, kb_l, ka_h, ka_l,
    send_sem, recv_sem, near_sem, detour_sem, local_sem, ready_sem,
):
    a, b = lax.axis_index("alpha"), lax.axis_index("beta")
    nz = nb // 2
    core, z = lax.rem(a, 2), lax.rem(b, nz)
    column = b - z
    low_wrap, high_wrap = z == 0, z == nz - 1
    wrap = jnp.logical_or(low_wrap, high_wrap)
    even = lax.rem(z, 2) == 0
    far_a, inner_b = lax.rem(a + 2 * core + na - 1, na), lax.rem(b + nz, nb)
    core_device = (a + 1 - 2 * core, b)
    inner_device = (a, inner_b)
    outer_device = (far_a, inner_b)
    far_device = (far_a, b)
    up_device = (a, column + lax.rem(z + 1, nz))
    down_device = (a, column + lax.rem(z + nz - 1, nz))

    own_copy = pltpu.make_async_copy(c_ref, own, local_sem.at[0])
    hb_copy = pltpu.make_async_copy(hb_ref, hb, local_sem.at[1])
    ha_copy = pltpu.make_async_copy(ha_ref, ha, local_sem.at[2])
    own_copy.start()
    hb_copy.start()
    ha_copy.start()

    def remote(source, target, flow, k, device):
        return pltpu.make_async_remote_copy(
            src_ref=source.at[chunk(k)],
            dst_ref=target.at[chunk(k)],
            send_sem=send_sem.at[flow, k],
            recv_sem=recv_sem.at[flow, k],
            device_id=device,
            device_id_type=MESH,
        )

    def to_inner(k):
        return remote(c_ref, relay, 0, k, inner_device)

    def to_far(k):
        return remote(c_ref, far, 1, k, far_device)

    def to_outer(k):
        return remote(relay, far, 1, k, outer_device)

    def to_up(k, source=c_ref):
        return remote(source, left, 2, k, up_device)

    def to_down(k, source=c_ref):
        return remote(source, right, 3, k, down_device)

    to_core = pltpu.make_async_remote_copy(
        src_ref=c_ref, dst_ref=near, send_sem=near_sem.at[0], recv_sem=near_sem.at[1],
        device_id=core_device, device_id_type=MESH,
    )
    to_detour = pltpu.make_async_remote_copy(
        src_ref=c_ref.at[chunk(FINAL)], dst_ref=detour,
        send_sem=send_sem.at[2, FINAL], recv_sem=detour_sem.at[0],
        device_id=up_device, device_id_type=MESH,
    )
    from_detour = pltpu.make_async_remote_copy(
        src_ref=detour, dst_ref=left.at[chunk(FINAL)],
        send_sem=detour_sem.at[1], recv_sem=recv_sem.at[2, FINAL],
        device_id=inner_device, device_id_type=MESH,
    )

    def each(body, first=0, last=CHUNKS):
        @pl.loop(first, min(last, EVEN))
        def _(k):
            body(k)

        for k in range(EVEN, last):
            body(k)

    barrier = pltpu.get_barrier_semaphore()
    for device in (core_device, inner_device, outer_device, far_device):
        pl.semaphore_signal(barrier, inc=1, device_id=device, device_id_type=MESH)

    @pl.when(even)
    def _():
        for device in (up_device, down_device):
            pl.semaphore_signal(barrier, inc=1, device_id=device, device_id_type=MESH)

    pl.semaphore_wait(barrier, jnp.where(even, 4, 6))

    @pl.when(jnp.logical_not(even))
    def _():
        for device in (up_device, down_device):
            pl.semaphore_signal(ready_sem, inc=1, device_id=device, device_id_type=MESH)

    @pl.when(wrap)
    def _():
        each(lambda k: to_inner(k).start(), last=FINAL)

    @pl.when(low_wrap)
    def _():
        to_inner(FINAL).start()

    @pl.when(jnp.logical_not(wrap))
    def _():
        each(lambda k: to_far(k).start(), last=FINAL)

    @pl.when(jnp.logical_not(low_wrap))
    def _():
        to_far(FINAL).start()

    @pl.when(even)
    def _():
        pl.semaphore_wait(ready_sem, 2)

    @pl.when(high_wrap)
    def _():
        to_detour.start()

    @pl.when(jnp.logical_not(high_wrap))
    def _():
        each(lambda k: to_up(k).start())

    @pl.when(jnp.logical_not(low_wrap))
    def _():
        each(lambda k: to_down(k).start())

    to_core.start()

    def forward(k):
        @pl.when(wrap)
        def _():
            to_inner(k).wait_recv()

        @pl.when(high_wrap)
        def _():
            to_up(k, relay).start()

        @pl.when(low_wrap)
        def _():
            to_down(k, relay).start()

        @pl.when(wrap)
        def _():
            to_outer(k).start()

    def select(blocks, links, counts, t, group, rows):
        total = None
        for l in range(LIST):
            used = jnp.logical_and(links[t, l] == group, l < counts[t])
            term = jnp.where(used, 1.0, 0.0) * blocks[t, l, rows, :]
            total = term if total is None else total + term
        return total

    def build(s):
        for t in range(GPD):
            beta_group = lax.rem(GPD * (b + nb - 1) + s, GPD * nb)
            alpha_group = lax.rem(GPD * (a + na - 1) + s, GPD * na)
            at = pl.multiple_of(s * G, 128)

            @pl.loop(0, G // 64)
            def _(i):
                rows = pl.ds(pl.multiple_of(i * 64, 64), 64)
                high, low = split(select(hb, lb_ref, cb_ref, t, beta_group, rows))
                to = (pl.ds(pl.multiple_of(at + i * 64, 64), 64), pl.ds(t * G, G))
                kb_h[to], kb_l[to] = high, low
                high, low = split(select(ha, la_ref, ca_ref, t, alpha_group, rows))
                to = (pl.ds(pl.multiple_of(t * G + i * 64, 64), 64), pl.ds(at, G))
                ka_h[to], ka_l[to] = high, low

        rows = pl.ds(pl.multiple_of(s * 128, 128), 128)
        own_h[rows, :], own_l[rows, :] = split(own[rows, :])

    def arrived(copy, first, last):
        @pl.loop(first, min(last, EVEN))
        def _(k):
            copy(k).wait_recv()

        for k in range(max(first, EVEN), last):
            copy(k).wait_recv()

    def side(block, at, first, size):
        rows, theirs = pl.ds(first, size), pl.ds(at, S)
        out_ref[rows, :] += product(*split(block[rows, :]), kb_h[theirs, :], kb_l[theirs, :])

    def sides(first, size):
        for copy, block, at in ((to_up, left, 0), (to_down, right, 2 * S)):
            arrived(copy, first // R, (first + size) // R)
            side(block, at, first, size)

    def outer(first, size):
        theirs = pl.ds(pl.multiple_of(far_at + first, 128), size)
        high, low = split(far[pl.ds(first, size), :])
        stacked = jnp.concatenate([high, high, low], axis=0)

        @pl.loop(0, 3)
        def _(i):
            block = pl.ds(pl.multiple_of(i * 256, 256), 256)
            high, low = ka_h[block, theirs], ka_l[block, theirs]
            wide = jnp.concatenate([high, low, high], axis=1)
            out_ref[block, :] += jnp.dot(wide, stacked, preferred_element_type=jnp.float32)

    near_at = jnp.where(core == 1, 0, 2 * S)
    far_at = 2 * S - near_at
    mine = pl.ds(S, S)

    def third(i):
        return pl.ds(pl.multiple_of(i * 256, 256), 256)

    own_copy.wait()
    hb_copy.wait()
    ha_copy.wait()

    @pl.loop(0, 2)
    def _(step):
        forward(step)

        @pl.loop(0, 3)
        def _(i):
            build(3 * step + i)

    forward(2)

    @pl.loop(0, 3)
    def _(i):
        rows = third(i)
        out_ref[rows, :] = product(own_h[rows, :], own_l[rows, :], kb_h[mine, :], kb_l[mine, :])

    forward(3)

    @pl.loop(0, 3)
    def _(i):
        rows = third(i)
        out_ref[rows, :] += product(ka_h[rows, mine], ka_l[rows, mine], own_h[...], own_l[...])

    forward(4)
    to_core.wait_recv()

    @pl.when(low_wrap)
    def _():
        to_detour.wait_recv()
        from_detour.start()

    @pl.loop(0, 3)
    def _(i):
        rows = third(i)
        near_h[rows, :], near_l[rows, :] = split(near[rows, :])

    forward(5)

    @pl.loop(0, 3)
    def _(i):
        rows = third(i)
        theirs = pl.ds(pl.multiple_of(near_at, 256), S)
        out_ref[rows, :] += product(ka_h[rows, theirs], ka_l[rows, theirs], near_h[...], near_l[...])

    forward(6)
    sides(0, 128)
    forward(7)
    sides(128, 128)
    forward(8)
    arrived(to_far, 0, 4)
    outer(0, 256)
    forward(9)
    sides(256, 128)
    forward(10)
    arrived(to_far, 4, 8)
    outer(256, 256)
    sides(384, 128)

    @pl.when(low_wrap)
    def _():
        forward(FINAL)

    sides(512, 128)
    arrived(to_far, 8, 10)
    outer(512, 128)

    to_core.wait_send()

    @pl.when(wrap)
    def _():
        each(lambda k: to_inner(k).wait_send(), last=FINAL)

    @pl.when(low_wrap)
    def _():
        to_inner(FINAL).wait_send()
        from_detour.wait_send()

    arrived(to_down, EVEN, CHUNKS)
    side(right, 2 * S, 640, 128)
    arrived(to_up, EVEN, CHUNKS)
    side(left, 0, 640, 128)
    arrived(to_far, EVEN, CHUNKS)
    outer(640, 128)

    each(lambda k: to_far(k).wait_send())
    each(lambda k: to_up(k).wait_send())
    each(lambda k: to_down(k).wait_send())


def store(total_ref, out_ref, sem):
    copy = pltpu.make_async_copy(total_ref, out_ref, sem)
    copy.start()
    copy.wait()


def solution(mesh):
    na, nb = mesh.shape["alpha"], mesh.shape["beta"]

    def on_device(
        coefficients, beta_blocks, alpha_blocks, beta_links, alpha_links, beta_count, alpha_count
    ):
        block = pltpu.VMEM((S, S), jnp.float32)
        listed = pltpu.VMEM((GPD, LIST, G, G), jnp.float32)
        half = pltpu.VMEM((S, S), jnp.bfloat16)
        tall = pltpu.VMEM((3 * S, S), jnp.bfloat16)
        wide = pltpu.VMEM((S, 3 * S), jnp.bfloat16)
        total = pl.pallas_call(
            functools.partial(kernel, na, nb),
            out_shape=pltpu.VMEM((S, S), jnp.float32),
            in_specs=[pl.BlockSpec(memory_space=pltpu.HBM)] * 3
            + [pl.BlockSpec(memory_space=pltpu.SMEM)] * 4,
            out_specs=pl.BlockSpec(memory_space=pltpu.VMEM),
            scratch_shapes=[block] * 6
            + [pltpu.VMEM((LAST, S), jnp.float32)]
            + [listed] * 2
            + [half] * 4
            + [tall, tall, wide, wide]
            + [
                pltpu.SemaphoreType.DMA((4, CHUNKS)),
                pltpu.SemaphoreType.DMA((4, CHUNKS)),
                pltpu.SemaphoreType.DMA((2,)),
                pltpu.SemaphoreType.DMA((2,)),
                pltpu.SemaphoreType.DMA((3,)),
                pltpu.SemaphoreType.REGULAR,
            ],
            compiler_params=pltpu.CompilerParams(
                collective_id=0, has_side_effects=True, vmem_limit_bytes=58 * 2**20
            ),
            name="sigma",
        )(
            coefficients, beta_blocks, alpha_blocks,
            beta_links, alpha_links, beta_count, alpha_count,
        )
        return pl.pallas_call(
            store,
            out_shape=jax.ShapeDtypeStruct((S, S), jnp.float32),
            in_specs=[pl.BlockSpec(memory_space=pltpu.VMEM)],
            out_specs=pl.BlockSpec(memory_space=pl.ANY),
            scratch_shapes=[pltpu.SemaphoreType.DMA],
            compiler_params=pltpu.CompilerParams(vmem_limit_bytes=8 * 2**20),
            name="store",
        )(total)

    return jax.shard_map(
        on_device,
        mesh=mesh,
        in_specs=(
            P("alpha", "beta"),
            P("beta", None, None, None),
            P("alpha", None, None, None),
            P("beta", None),
            P("alpha", None),
            P("beta"),
            P("alpha"),
        ),
        out_specs=P("alpha", "beta"),
        check_vma=False,
    )
```

```python
import functools

import jax
import jax.numpy as jnp
from jax import lax
from jax.experimental import pallas as pl
from jax.experimental.pallas import tpu as pltpu
from jax.sharding import PartitionSpec as P

MESH = pl.DeviceIdType.MESH
G = 384
GPD = 2
LIST = 3
S = G * GPD
R = 64
EVEN = 10
REST = ((640, 32), (672, 64), (736, 32))
CHUNKS = EVEN + len(REST)
DETOUR = EVEN + 1
STORES = 6
TAIL = 128


def split(x):
    high = x.astype(jnp.bfloat16)
    return high, (x - high.astype(jnp.float32)).astype(jnp.bfloat16)


def product(a_high, a_low, b_high, b_low):
    dot = functools.partial(jnp.dot, preferred_element_type=jnp.float32)
    return dot(a_high, b_high) + dot(a_low, b_high) + dot(a_high, b_low)


def chunk(k):
    if isinstance(k, int) and k >= EVEN:
        return pl.ds(*REST[k - EVEN])
    return pl.ds(k * R, R)


def kernel(
    na, nb,
    c_ref, hb_ref, ha_ref, lb_in, la_in, cb_in, ca_in,
    out_ref, wide_ref, stacked_ref,
    lb_ref, la_ref, cb_ref, ca_ref, own, near, far, left, right, relay, detour, hb, ha,
    own_h, own_l, near_h, near_l, kb_h, kb_l, ka_h, ka_l,
    send_sem, recv_sem, near_sem, detour_sem, local_sem, ready_sem,
):
    a, b = lax.axis_index("alpha"), lax.axis_index("beta")
    nz = nb // 2
    core, z = lax.rem(a, 2), lax.rem(b, nz)

    def turned(a):
        return a + 2 - 4 * lax.rem(a // 2, 2)

    column = b - z
    low_wrap, high_wrap = z == 0, z == nz - 1
    wrap = jnp.logical_or(low_wrap, high_wrap)
    even = lax.rem(z, 2) == 0
    far_a, inner_b = lax.rem(a + 2 * core + na - 1, na), lax.rem(b + nz, nb)
    core_device = (a + 1 - 2 * core, b)
    inner_device = (a, inner_b)
    outer_device = (far_a, inner_b)
    far_device = (far_a, b)
    other_a = turned(a)
    skip_device = (other_a, inner_b)
    skipped_device = (lax.rem(other_a + 2 * core + na - 1, na), inner_b)
    skipping_device = (turned(far_a), inner_b)
    up_device = (a, column + lax.rem(z + 1, nz))
    down_device = (a, column + lax.rem(z + nz - 1, nz))

    loads = [
        pltpu.make_async_copy(source, target, local_sem.at[i])
        for i, (source, target) in enumerate(
            (
                (lb_in, lb_ref), (la_in, la_ref), (cb_in, cb_ref), (ca_in, ca_ref),
                (hb_ref, hb), (ha_ref, ha), (c_ref, own),
            )
        )
    ]

    def remote(source, target, flow, k, device):
        return pltpu.make_async_remote_copy(
            src_ref=source.at[chunk(k)],
            dst_ref=target.at[chunk(k)],
            send_sem=send_sem.at[flow, k],
            recv_sem=recv_sem.at[flow, k],
            device_id=device,
            device_id_type=MESH,
        )

    def to_inner(k):
        return remote(c_ref, relay, 0, k, inner_device)

    def to_far(k):
        return remote(c_ref, far, 1, k, far_device)

    def to_outer(k):
        return remote(relay, far, 1, k, outer_device)

    def to_up(k, source=c_ref):
        return remote(source, left, 2, k, up_device)

    def to_down(k, source=c_ref):
        return remote(source, right, 3, k, down_device)

    to_core = pltpu.make_async_remote_copy(
        src_ref=c_ref, dst_ref=near, send_sem=near_sem.at[0], recv_sem=near_sem.at[1],
        device_id=core_device, device_id_type=MESH,
    )

    def held(k):
        first, size = REST[k - EVEN]
        return detour.at[pl.ds(first - REST[1][0], size)]

    def to_detour(k):
        return pltpu.make_async_remote_copy(
            src_ref=c_ref.at[chunk(k)], dst_ref=held(k),
            send_sem=send_sem.at[2, k], recv_sem=detour_sem.at[0, k - DETOUR],
            device_id=up_device, device_id_type=MESH,
        )

    def from_detour(k):
        return pltpu.make_async_remote_copy(
            src_ref=held(k), dst_ref=left.at[chunk(k)],
            send_sem=detour_sem.at[1, k - DETOUR], recv_sem=recv_sem.at[2, k],
            device_id=inner_device, device_id_type=MESH,
        )

    def to_skip(k):
        return pltpu.make_async_remote_copy(
            src_ref=c_ref.at[chunk(k)], dst_ref=held(k),
            send_sem=send_sem.at[1, k], recv_sem=detour_sem.at[0, k - DETOUR],
            device_id=skip_device, device_id_type=MESH,
        )

    def from_skip(k):
        return pltpu.make_async_remote_copy(
            src_ref=held(k), dst_ref=far.at[chunk(k)],
            send_sem=detour_sem.at[1, k - DETOUR], recv_sem=recv_sem.at[1, k],
            device_id=skipped_device, device_id_type=MESH,
        )

    def each(body, first=0, last=CHUNKS):
        if first < EVEN:

            @pl.loop(first, min(last, EVEN))
            def _(k):
                body(k)

        for k in range(max(first, EVEN), last):
            body(k)

    barrier = pltpu.get_barrier_semaphore()
    for device in (core_device, inner_device, outer_device, far_device):
        pl.semaphore_signal(barrier, inc=1, device_id=device, device_id_type=MESH)

    @pl.when(even)
    def _():
        for device in (up_device, down_device):
            pl.semaphore_signal(barrier, inc=1, device_id=device, device_id_type=MESH)

    @pl.when(high_wrap)
    def _():
        for device in (skip_device, skipped_device, skipping_device):
            pl.semaphore_signal(barrier, inc=1, device_id=device, device_id_type=MESH)

    for load in loads:
        load.start()

    pl.semaphore_wait(barrier, jnp.where(even, 4, jnp.where(high_wrap, 9, 6)))

    @pl.when(jnp.logical_not(even))
    def _():
        for device in (up_device, down_device):
            pl.semaphore_signal(ready_sem, inc=1, device_id=device, device_id_type=MESH)

    @pl.when(wrap)
    def _():
        each(lambda k: to_inner(k).start(), last=DETOUR)

    @pl.when(low_wrap)
    def _():
        each(lambda k: to_inner(k).start(), first=DETOUR)

    @pl.when(jnp.logical_not(wrap))
    def _():
        each(lambda k: to_far(k).start())

    @pl.when(high_wrap)
    def _():
        each(lambda k: to_skip(k).start(), first=DETOUR)

    to_core.start()

    @pl.when(even)
    def _():
        pl.semaphore_wait(ready_sem, 2)

    @pl.when(high_wrap)
    def _():
        each(lambda k: to_detour(k).start(), first=DETOUR)

    @pl.when(jnp.logical_not(high_wrap))
    def _():
        each(lambda k: to_up(k).start())

    @pl.when(jnp.logical_not(low_wrap))
    def _():
        each(lambda k: to_down(k).start())

    def forward(k):
        @pl.when(wrap)
        def _():
            to_inner(k).wait_recv()

        @pl.when(high_wrap)
        def _():
            to_up(k, relay).start()

        @pl.when(low_wrap)
        def _():
            to_down(k, relay).start()

        @pl.when(wrap)
        def _():
            to_outer(k).start()

    near_at = jnp.where(core == 1, 0, 2 * S)
    far_at = 2 * S - near_at
    mine = pl.ds(S, S)

    def third(i):
        return pl.ds(pl.multiple_of(i * 256, 256), 256)

    def select(blocks, links, counts, t, group, rows):
        total = None
        for l in range(LIST):
            used = jnp.logical_and(links[t, l] == group, l < counts[t])
            term = jnp.where(used, 1.0, 0.0) * blocks[t, l, rows, :]
            total = term if total is None else total + term
        return total

    def build(s):
        for t in range(GPD):
            beta_group = lax.rem(GPD * (b + nb - 1) + s, GPD * nb)
            alpha_group = lax.rem(GPD * (a + na - 1) + s, GPD * na)
            at = pl.multiple_of(s * G, 128)

            @pl.loop(0, G // 64)
            def _(i):
                rows = pl.ds(pl.multiple_of(i * 64, 64), 64)
                high, low = split(select(hb, lb_ref, cb_ref, t, beta_group, rows))
                to = (pl.ds(pl.multiple_of(at + i * 64, 64), 64), pl.ds(t * G, G))
                kb_h[to], kb_l[to] = high, low
                high, low = split(select(ha, la_ref, ca_ref, t, alpha_group, rows))
                to = (pl.ds(pl.multiple_of(t * G + i * 64, 64), 64), pl.ds(at, G))
                ka_h[to], ka_l[to] = high, low

        rows = pl.ds(pl.multiple_of(s * 128, 128), 128)
        own_h[rows, :], own_l[rows, :] = split(own[rows, :])

    def arrived(copy, first, last):
        each(lambda k: copy(k).wait_recv(), first, last)

    def side(block, at, first, size):
        rows, theirs = pl.ds(first, size), pl.ds(at, S)
        out_ref[rows, :] += product(*split(block[rows, :]), kb_h[theirs, :], kb_l[theirs, :])

    def sides(first, size):
        for copy, block, at in ((to_up, left, 0), (to_down, right, 2 * S)):
            arrived(copy, first // R, (first + size) // R)
            side(block, at, first, size)

    def stack(first, size):
        high, low = split(far[pl.ds(first, size), :])
        return jnp.concatenate([high, high, low], axis=0)

    def widen(block, first, size):
        theirs = pl.ds(pl.multiple_of(far_at + first, 128), size)
        high, low = ka_h[block, theirs], ka_l[block, theirs]
        return jnp.concatenate([high, low, high], axis=1)

    def outer(first, size):
        stacked = stack(first, size)

        @pl.loop(0, 3)
        def _(i):
            block = third(i)
            wide = widen(block, first, size)
            out_ref[block, :] += jnp.dot(wide, stacked, preferred_element_type=jnp.float32)

    for load in loads:
        load.wait()

    @pl.loop(0, 2)
    def _(step):
        forward(step)

        @pl.loop(0, 3)
        def _(i):
            build(3 * step + i)

    forward(2)

    @pl.loop(0, 3)
    def _(i):
        rows = third(i)
        out_ref[rows, :] = product(own_h[rows, :], own_l[rows, :], kb_h[mine, :], kb_l[mine, :])

    forward(3)

    @pl.loop(0, 3)
    def _(i):
        rows = third(i)
        out_ref[rows, :] += product(ka_h[rows, mine], ka_l[rows, mine], own_h[...], own_l[...])

    forward(4)
    to_core.wait_recv()

    @pl.when(low_wrap)
    def _():
        for k in range(DETOUR, CHUNKS):
            to_detour(k).wait_recv()
            from_detour(k).start()

    @pl.when(high_wrap)
    def _():
        for k in range(DETOUR, CHUNKS):
            to_skip(k).wait_recv()
            from_skip(k).start()

    @pl.loop(0, 3)
    def _(i):
        rows = third(i)
        near_h[rows, :], near_l[rows, :] = split(near[rows, :])
        wide_ref[rows, :] = widen(rows, S - TAIL, TAIL)

    forward(5)

    @pl.loop(0, 3)
    def _(i):
        rows = third(i)
        theirs = pl.ds(pl.multiple_of(near_at, 256), S)
        out_ref[rows, :] += product(ka_h[rows, theirs], ka_l[rows, theirs], near_h[...], near_l[...])

    forward(6)
    sides(0, 128)
    forward(7)
    sides(128, 128)
    forward(8)
    arrived(to_far, 0, 4)
    outer(0, 256)
    forward(9)
    sides(256, 128)
    forward(10)
    arrived(to_far, 4, 8)
    outer(256, 256)
    sides(384, 128)

    @pl.when(low_wrap)
    def _():
        for k in range(DETOUR, CHUNKS):
            forward(k)

    sides(512, 128)
    arrived(to_far, 8, 10)
    outer(512, 128)

    to_core.wait_send()

    @pl.when(wrap)
    def _():
        each(lambda k: to_inner(k).wait_send(), last=DETOUR)

    @pl.when(low_wrap)
    def _():
        for k in range(DETOUR, CHUNKS):
            to_inner(k).wait_send()
            from_detour(k).wait_send()

    @pl.when(high_wrap)
    def _():
        for k in range(DETOUR, CHUNKS):
            from_skip(k).wait_send()

    arrived(to_down, EVEN, CHUNKS)
    side(right, 2 * S, 640, 128)
    arrived(to_up, EVEN, CHUNKS)
    side(left, 0, 640, 128)
    arrived(to_far, EVEN, CHUNKS)
    stacked_ref[...] = stack(S - TAIL, TAIL)

    each(lambda k: to_far(k).wait_send())
    each(lambda k: to_up(k).wait_send())
    each(lambda k: to_down(k).wait_send())


def store(total_ref, wide_ref, stacked_ref, out_ref, result, sem):
    size = S // STORES
    copies = []
    for i in range(STORES):
        rows = pl.ds(i * size, size)
        result[rows, :] = total_ref[rows, :] + jnp.dot(
            wide_ref[rows, :], stacked_ref[...], preferred_element_type=jnp.float32
        )
        copies.append(pltpu.make_async_copy(result.at[rows], out_ref.at[rows], sem.at[i]))
        copies[-1].start()
    for copy in copies:
        copy.wait()


def solution(mesh):
    na, nb = mesh.shape["alpha"], mesh.shape["beta"]

    def on_device(
        coefficients, beta_blocks, alpha_blocks, beta_links, alpha_links, beta_count, alpha_count
    ):
        block = pltpu.VMEM((S, S), jnp.float32)
        listed = pltpu.VMEM((GPD, LIST, G, G), jnp.float32)
        half = pltpu.VMEM((S, S), jnp.bfloat16)
        tall = pltpu.VMEM((3 * S, S), jnp.bfloat16)
        wide = pltpu.VMEM((S, 3 * S), jnp.bfloat16)
        total, wide_rows, stacked = pl.pallas_call(
            functools.partial(kernel, na, nb),
            out_shape=(
                pltpu.VMEM((S, S), jnp.float32),
                pltpu.VMEM((S, 3 * TAIL), jnp.bfloat16),
                pltpu.VMEM((3 * TAIL, S), jnp.bfloat16),
            ),
            in_specs=[pl.BlockSpec(memory_space=pltpu.HBM)] * 7,
            out_specs=[pl.BlockSpec(memory_space=pltpu.VMEM)] * 3,
            scratch_shapes=[pltpu.SMEM((GPD, LIST), jnp.int32)] * 2
            + [pltpu.SMEM((GPD,), jnp.int32)] * 2
            + [block] * 6
            + [pltpu.VMEM((S - REST[1][0], S), jnp.float32)]
            + [listed] * 2
            + [half] * 4
            + [tall, tall, wide, wide]
            + [
                pltpu.SemaphoreType.DMA((4, CHUNKS)),
                pltpu.SemaphoreType.DMA((4, CHUNKS)),
                pltpu.SemaphoreType.DMA((2,)),
                pltpu.SemaphoreType.DMA((2, 2)),
                pltpu.SemaphoreType.DMA((7,)),
                pltpu.SemaphoreType.REGULAR,
            ],
            compiler_params=pltpu.CompilerParams(
                collective_id=0, has_side_effects=True, vmem_limit_bytes=58 * 2**20
            ),
            name="sigma",
        )(
            coefficients, beta_blocks, alpha_blocks,
            beta_links, alpha_links, beta_count, alpha_count,
        )
        return pl.pallas_call(
            store,
            out_shape=jax.ShapeDtypeStruct((S, S), jnp.float32),
            in_specs=[pl.BlockSpec(memory_space=pltpu.VMEM)] * 3,
            out_specs=pl.BlockSpec(memory_space=pl.ANY),
            scratch_shapes=[block, pltpu.SemaphoreType.DMA((STORES,))],
            compiler_params=pltpu.CompilerParams(vmem_limit_bytes=8 * 2**20),
            name="store",
        )(total, wide_rows, stacked)

    return jax.shard_map(
        on_device,
        mesh=mesh,
        in_specs=(
            P("alpha", "beta"),
            P("beta", None, None, None),
            P("alpha", None, None, None),
            P("beta", None),
            P("alpha", None),
            P("beta"),
            P("alpha"),
        ),
        out_specs=P("alpha", "beta"),
        check_vma=False,
    )
```

```python
import functools

import jax
import jax.numpy as jnp
from jax import lax
from jax.experimental import pallas as pl
from jax.experimental.pallas import tpu as pltpu
from jax.sharding import PartitionSpec as P

MESH = pl.DeviceIdType.MESH
G = 384
GPD = 2
LIST = 3
S = G * GPD
R = 64
EVEN = 10
REST = ((640, 32), (672, 64), (736, 32))
CHUNKS = EVEN + len(REST)
DETOUR = EVEN + 1
LAST = S - REST[1][0]
FAR = ((0, 256), (256, 256), (512, 128), (640, 128))
STORES = 6
TAIL = 128
SIDES = S // TAIL


def split(x):
    high = x.astype(jnp.bfloat16)
    return high, (x - high.astype(jnp.float32)).astype(jnp.bfloat16)


def product(a_high, a_low, b_high, b_low):
    dot = functools.partial(jnp.dot, preferred_element_type=jnp.float32)
    return dot(a_high, b_high) + dot(a_low, b_high) + dot(a_high, b_low)


def chunk(k):
    if isinstance(k, int) and k >= EVEN:
        return pl.ds(*REST[k - EVEN])
    return pl.ds(k * R, R)


def kernel(
    na, nb,
    c_ref, hb_ref, ha_ref, lb_in, la_in, cb_in, ca_in,
    out_ref, wide_ref, stacked_ref,
    lb_ref, la_ref, cb_ref, ca_ref, own, near, far, left, right, relay, detour, hb, ha,
    own_h, own_l, near_h, near_l, kb_h, kb_l, ka_h, ka_l,
    send_sem, relay_sem, far_sem, left_sem, right_sem, near_sem, detour_sem, local_sem, ready_sem,
):
    a, b = lax.axis_index("alpha"), lax.axis_index("beta")
    nz = nb // 2
    core, z = lax.rem(a, 2), lax.rem(b, nz)

    def turned(a):
        return a + 2 - 4 * lax.rem(a // 2, 2)

    column = b - z
    low_wrap, high_wrap = z == 0, z == nz - 1
    wrap = jnp.logical_or(low_wrap, high_wrap)
    even = lax.rem(z, 2) == 0
    far_a, inner_b = lax.rem(a + 2 * core + na - 1, na), lax.rem(b + nz, nb)
    core_device = (a + 1 - 2 * core, b)
    inner_device = (a, inner_b)
    outer_device = (far_a, inner_b)
    far_device = (far_a, b)
    other_a = turned(a)
    skip_device = (other_a, inner_b)
    skipped_device = (lax.rem(other_a + 2 * core + na - 1, na), inner_b)
    skipping_device = (turned(far_a), inner_b)
    up_device = (a, column + lax.rem(z + 1, nz))
    down_device = (a, column + lax.rem(z + nz - 1, nz))

    loads = [
        pltpu.make_async_copy(source, target, local_sem.at[i])
        for i, (source, target) in enumerate(
            (
                (lb_in, lb_ref), (la_in, la_ref), (cb_in, cb_ref), (ca_in, ca_ref),
                (hb_ref, hb), (ha_ref, ha), (c_ref, own),
            )
        )
    ]

    whole, most, last = pl.ds(0, S), pl.ds(0, S - LAST), pl.ds(S - LAST, LAST)

    def remote(source, target, send, recv, device):
        return pltpu.make_async_remote_copy(
            src_ref=source, dst_ref=target, send_sem=send, recv_sem=recv,
            device_id=device, device_id_type=MESH,
        )

    def to_inner(rows, k):
        source, target = c_ref.at[rows], relay.at[rows]
        return remote(source, target, send_sem.at[0], relay_sem.at[k], inner_device)

    def to_far(rows, at, source=c_ref, device=far_device):
        return remote(source.at[rows], far.at[rows], send_sem.at[1], far_sem.at[at], device)

    def to_up(rows, at, source=c_ref):
        return remote(source.at[rows], left.at[rows], send_sem.at[2], left_sem.at[at], up_device)

    def to_down(rows, at, source=c_ref):
        source, target = source.at[rows], right.at[rows]
        return remote(source, target, send_sem.at[3], right_sem.at[at], down_device)

    to_core = remote(c_ref, near, near_sem.at[0], near_sem.at[1], core_device)
    mine_last = c_ref.at[last]
    to_detour = remote(mine_last, detour, send_sem.at[2], detour_sem.at[0], up_device)
    to_skip = remote(mine_last, detour, send_sem.at[1], detour_sem.at[0], skip_device)
    from_detour = remote(
        detour, left.at[last], detour_sem.at[1], left_sem.at[SIDES - 1], inner_device
    )
    from_skip = remote(
        detour, far.at[last], detour_sem.at[1], far_sem.at[len(FAR) - 1], skipped_device
    )

    def each(body, chunks):
        @pl.loop(0, EVEN)
        def _(k):
            body(k)

        for k in range(EVEN, chunks):
            body(k)

    def side_rows(p):
        return pl.ds(pl.multiple_of(p * TAIL, TAIL), TAIL)

    barrier = pltpu.get_barrier_semaphore()

    def greet(*devices):
        for device in devices:
            pl.semaphore_signal(barrier, inc=1, device_id=device, device_id_type=MESH)

    greet(core_device)
    pl.when(wrap)(lambda: greet(inner_device, outer_device))
    pl.when(jnp.logical_not(wrap))(lambda: greet(far_device))
    pl.when(even)(lambda: greet(up_device, down_device))
    pl.when(high_wrap)(lambda: greet(skip_device, skipped_device, skipping_device))

    for load in loads:
        load.start()

    pl.semaphore_wait(barrier, jnp.where(wrap, 3, 2) + jnp.where(even, 0, 2) + jnp.where(high_wrap, 3, 0))

    @pl.when(jnp.logical_not(even))
    def _():
        for device in (up_device, down_device):
            pl.semaphore_signal(ready_sem, inc=1, device_id=device, device_id_type=MESH)

    @pl.when(wrap)
    def _():
        each(lambda k: to_inner(chunk(k), k).start(), DETOUR)

    @pl.when(low_wrap)
    def _():
        for k in range(DETOUR, CHUNKS):
            to_inner(chunk(k), k).start()

    @pl.when(jnp.logical_not(wrap))
    def _():
        for at, rows in enumerate(FAR):
            to_far(pl.ds(*rows), at).start()

    @pl.when(high_wrap)
    def _():
        to_skip.start()

    @pl.when(even)
    def _():
        pl.semaphore_wait(ready_sem, 2)

    @pl.when(high_wrap)
    def _():
        to_detour.start()

    @pl.when(jnp.logical_not(high_wrap))
    def _():
        @pl.loop(0, SIDES)
        def _(p):
            to_up(side_rows(p), p).start()

    @pl.when(jnp.logical_not(low_wrap))
    def _():
        @pl.loop(0, SIDES)
        def _(p):
            to_down(side_rows(p), p).start()

    def forward(k):
        rows = chunk(k)
        rest = isinstance(k, int) and k >= EVEN
        side_at, far_block = (SIDES - 1, len(FAR) - 1) if rest else (k // 2, k // 4)

        @pl.when(wrap)
        def _():
            to_inner(rows, k).wait_recv()

        @pl.when(high_wrap)
        def _():
            to_up(rows, side_at, relay).start()

        @pl.when(low_wrap)
        def _():
            to_down(rows, side_at, relay).start()

        @pl.when(wrap)
        def _():
            to_outer = to_far(rows, far_block, relay, outer_device)
            to_outer.start()

    near_at = jnp.where(core == 1, 0, 2 * S)
    far_at = 2 * S - near_at
    mine = pl.ds(S, S)

    def third(i):
        return pl.ds(pl.multiple_of(i * 256, 256), 256)

    def select(blocks, links, counts, t, group, rows):
        total = None
        for l in range(LIST):
            used = jnp.logical_and(links[t, l] == group, l < counts[t])
            term = jnp.where(used, 1.0, 0.0) * blocks[t, l, rows, :]
            total = term if total is None else total + term
        return total

    def build(s):
        for t in range(GPD):
            beta_group = lax.rem(GPD * (b + nb - 1) + s, GPD * nb)
            alpha_group = lax.rem(GPD * (a + na - 1) + s, GPD * na)
            at = pl.multiple_of(s * G, 128)

            @pl.loop(0, G // 64)
            def _(i):
                rows = pl.ds(pl.multiple_of(i * 64, 64), 64)
                high, low = split(select(hb, lb_ref, cb_ref, t, beta_group, rows))
                to = (pl.ds(pl.multiple_of(at + i * 64, 64), 64), pl.ds(t * G, G))
                kb_h[to], kb_l[to] = high, low
                high, low = split(select(ha, la_ref, ca_ref, t, alpha_group, rows))
                to = (pl.ds(pl.multiple_of(t * G + i * 64, 64), 64), pl.ds(at, G))
                ka_h[to], ka_l[to] = high, low

        rows = pl.ds(pl.multiple_of(s * 128, 128), 128)
        own_h[rows, :], own_l[rows, :] = split(own[rows, :])

    def side(copy, block, at, p):
        rows, theirs = side_rows(p), pl.ds(at, S)
        copy(rows, p).wait_recv()
        out_ref[rows, :] += product(*split(block[rows, :]), kb_h[theirs, :], kb_l[theirs, :])

    def sides(p):
        side(to_down, right, 2 * S, p)
        side(to_up, left, 0, p)

    def stack(at):
        first, size = FAR[at]
        to_far(pl.ds(first, size), at).wait_recv()
        high, low = split(far[pl.ds(first, size), :])
        return jnp.concatenate([high, high, low], axis=0)

    def widen(block, first, size):
        theirs = pl.ds(pl.multiple_of(far_at + first, 128), size)
        high, low = ka_h[block, theirs], ka_l[block, theirs]
        return jnp.concatenate([high, low, high], axis=1)

    def outer(at):
        first, size = FAR[at]
        stacked = stack(at)

        @pl.loop(0, 3)
        def _(i):
            block = third(i)
            wide = widen(block, first, size)
            out_ref[block, :] += jnp.dot(wide, stacked, preferred_element_type=jnp.float32)

    for load in loads:
        load.wait()

    @pl.loop(0, 2)
    def _(step):
        forward(step)

        @pl.loop(0, 3)
        def _(i):
            build(3 * step + i)

    forward(2)
    to_core.start()

    @pl.loop(0, 3)
    def _(i):
        rows = third(i)
        out_ref[rows, :] = product(own_h[rows, :], own_l[rows, :], kb_h[mine, :], kb_l[mine, :])

    forward(3)

    @pl.loop(0, 3)
    def _(i):
        rows = third(i)
        out_ref[rows, :] += product(ka_h[rows, mine], ka_l[rows, mine], own_h[...], own_l[...])

    forward(4)
    to_core.wait_recv()

    @pl.when(low_wrap)
    def _():
        to_detour.wait_recv()
        from_detour.start()

    @pl.when(high_wrap)
    def _():
        to_skip.wait_recv()
        from_skip.start()

    @pl.loop(0, 3)
    def _(i):
        rows = third(i)
        near_h[rows, :], near_l[rows, :] = split(near[rows, :])
        wide_ref[rows, :] = widen(rows, S - TAIL, TAIL)

    forward(5)

    @pl.loop(0, 3)
    def _(i):
        rows = third(i)
        theirs = pl.ds(pl.multiple_of(near_at, 256), S)
        out_ref[rows, :] += product(ka_h[rows, theirs], ka_l[rows, theirs], near_h[...], near_l[...])

    forward(6)
    sides(0)
    forward(7)
    sides(1)
    forward(8)
    outer(0)
    forward(9)
    sides(2)
    forward(EVEN)
    outer(1)

    @pl.when(low_wrap)
    def _():
        forward(DETOUR)

    sides(3)

    @pl.when(low_wrap)
    def _():
        forward(DETOUR + 1)

    sides(4)
    outer(2)
    to_core.wait_send()
    sides(SIDES - 1)
    stacked_ref[...] = stack(len(FAR) - 1)

    @pl.when(high_wrap)
    def _():
        to_inner(most, 0).wait_send()

    @pl.when(low_wrap)
    def _():
        to_inner(whole, 0).wait_send()

    @pl.when(wrap)
    def _():
        from_detour.wait_send()

    to_far(whole, 0).wait_send()
    to_up(whole, 0).wait_send()
    to_down(whole, 0).wait_send()


def store(total_ref, wide_ref, stacked_ref, out_ref, result, sem):
    size = S // STORES
    copies = []
    for i in range(STORES):
        rows = pl.ds(i * size, size)
        result[rows, :] = total_ref[rows, :] + jnp.dot(
            wide_ref[rows, :], stacked_ref[...], preferred_element_type=jnp.float32
        )
        copies.append(pltpu.make_async_copy(result.at[rows], out_ref.at[rows], sem.at[i]))
        copies[-1].start()
    for copy in copies:
        copy.wait()


def solution(mesh):
    na, nb = mesh.shape["alpha"], mesh.shape["beta"]

    def on_device(
        coefficients, beta_blocks, alpha_blocks, beta_links, alpha_links, beta_count, alpha_count
    ):
        block = pltpu.VMEM((S, S), jnp.float32)
        listed = pltpu.VMEM((GPD, LIST, G, G), jnp.float32)
        half = pltpu.VMEM((S, S), jnp.bfloat16)
        tall = pltpu.VMEM((3 * S, S), jnp.bfloat16)
        wide = pltpu.VMEM((S, 3 * S), jnp.bfloat16)
        total, wide_rows, stacked = pl.pallas_call(
            functools.partial(kernel, na, nb),
            out_shape=(
                pltpu.VMEM((S, S), jnp.float32),
                pltpu.VMEM((S, 3 * TAIL), jnp.bfloat16),
                pltpu.VMEM((3 * TAIL, S), jnp.bfloat16),
            ),
            in_specs=[pl.BlockSpec(memory_space=pltpu.HBM)] * 7,
            out_specs=[pl.BlockSpec(memory_space=pltpu.VMEM)] * 3,
            scratch_shapes=[pltpu.SMEM((GPD, LIST), jnp.int32)] * 2
            + [pltpu.SMEM((GPD,), jnp.int32)] * 2
            + [block] * 6
            + [pltpu.VMEM((LAST, S), jnp.float32)]
            + [listed] * 2
            + [half] * 4
            + [tall, tall, wide, wide]
            + [
                pltpu.SemaphoreType.DMA((4,)),
                pltpu.SemaphoreType.DMA((CHUNKS,)),
                pltpu.SemaphoreType.DMA((len(FAR),)),
                pltpu.SemaphoreType.DMA((SIDES,)),
                pltpu.SemaphoreType.DMA((SIDES,)),
                pltpu.SemaphoreType.DMA((2,)),
                pltpu.SemaphoreType.DMA((2,)),
                pltpu.SemaphoreType.DMA((7,)),
                pltpu.SemaphoreType.REGULAR,
            ],
            compiler_params=pltpu.CompilerParams(
                collective_id=0, has_side_effects=True, vmem_limit_bytes=58 * 2**20
            ),
            name="sigma",
        )(
            coefficients, beta_blocks, alpha_blocks,
            beta_links, alpha_links, beta_count, alpha_count,
        )
        return pl.pallas_call(
            store,
            out_shape=jax.ShapeDtypeStruct((S, S), jnp.float32),
            in_specs=[pl.BlockSpec(memory_space=pltpu.VMEM)] * 3,
            out_specs=pl.BlockSpec(memory_space=pl.ANY),
            scratch_shapes=[block, pltpu.SemaphoreType.DMA((STORES,))],
            compiler_params=pltpu.CompilerParams(vmem_limit_bytes=8 * 2**20),
            name="store",
        )(total, wide_rows, stacked)

    return jax.shard_map(
        on_device,
        mesh=mesh,
        in_specs=(
            P("alpha", "beta"),
            P("beta", None, None, None),
            P("alpha", None, None, None),
            P("beta", None),
            P("alpha", None),
            P("beta"),
            P("alpha"),
        ),
        out_specs=P("alpha", "beta"),
        check_vma=False,
    )
```

```python
import functools

import jax
import jax.numpy as jnp
from jax import lax
from jax.experimental import pallas as pl
from jax.experimental.pallas import tpu as pltpu
from jax.sharding import PartitionSpec as P

MESH = pl.DeviceIdType.MESH
G = 384
GPD = 2
LIST = 3
S = G * GPD
R = 64
EVEN = 10
REST = ((640, 48), (688, 48), (736, 32))
CHUNKS = EVEN + len(REST)
DETOUR = EVEN + 1
LAST = S - REST[1][0]
FAR = ((0, 256), (256, 256), (512, 128), (640, 128))
STORES = 6
TAIL = 128
SIDES = S // TAIL


def split(x):
    high = x.astype(jnp.bfloat16)
    return high, (x - high.astype(jnp.float32)).astype(jnp.bfloat16)


def product(a_high, a_low, b_high, b_low):
    dot = functools.partial(jnp.dot, preferred_element_type=jnp.float32)
    return dot(a_high, b_high) + dot(a_low, b_high) + dot(a_high, b_low)


def chunk(k):
    if isinstance(k, int) and k >= EVEN:
        return pl.ds(*REST[k - EVEN])
    return pl.ds(k * R, R)


def kernel(
    na, nb,
    c_ref, hb_ref, ha_ref, lb_in, la_in, cb_in, ca_in,
    out_ref, wide_ref, stacked_ref,
    lb_ref, la_ref, cb_ref, ca_ref, own, near, far, left, right, relay, detour, hb, ha,
    own_h, own_l, near_h, near_l, kb_h, kb_l, ka_h, ka_l,
    send_sem, relay_sem, far_sem, left_sem, right_sem, near_sem, detour_sem, local_sem, ready_sem,
):
    a, b = lax.axis_index("alpha"), lax.axis_index("beta")
    nz = nb // 2
    core, z = lax.rem(a, 2), lax.rem(b, nz)

    def turned(a):
        return a + 2 - 4 * lax.rem(a // 2, 2)

    column = b - z
    low_wrap, high_wrap = z == 0, z == nz - 1
    wrap = jnp.logical_or(low_wrap, high_wrap)
    even = lax.rem(z, 2) == 0
    far_a, inner_b = lax.rem(a + 2 * core + na - 1, na), lax.rem(b + nz, nb)
    core_device = (a + 1 - 2 * core, b)
    inner_device = (a, inner_b)
    outer_device = (far_a, inner_b)
    far_device = (far_a, b)
    other_a = turned(a)
    skip_device = (other_a, inner_b)
    skipped_device = (lax.rem(other_a + 2 * core + na - 1, na), inner_b)
    skipping_device = (turned(far_a), inner_b)
    up_device = (a, column + lax.rem(z + 1, nz))
    down_device = (a, column + lax.rem(z + nz - 1, nz))

    loads = [
        pltpu.make_async_copy(source, target, local_sem.at[i])
        for i, (source, target) in enumerate(
            (
                (lb_in, lb_ref), (la_in, la_ref), (cb_in, cb_ref), (ca_in, ca_ref),
                (hb_ref, hb), (ha_ref, ha), (c_ref, own),
            )
        )
    ]

    whole, most, last = pl.ds(0, S), pl.ds(0, S - LAST), pl.ds(S - LAST, LAST)

    def remote(source, target, send, recv, device):
        return pltpu.make_async_remote_copy(
            src_ref=source, dst_ref=target, send_sem=send, recv_sem=recv,
            device_id=device, device_id_type=MESH,
        )

    def to_inner(rows, k):
        source, target = c_ref.at[rows], relay.at[rows]
        return remote(source, target, send_sem.at[0], relay_sem.at[k], inner_device)

    def to_far(rows, at, source=c_ref, device=far_device):
        return remote(source.at[rows], far.at[rows], send_sem.at[1], far_sem.at[at], device)

    def to_up(rows, at, source=c_ref):
        return remote(source.at[rows], left.at[rows], send_sem.at[2], left_sem.at[at], up_device)

    def to_down(rows, at, source=c_ref):
        source, target = source.at[rows], right.at[rows]
        return remote(source, target, send_sem.at[3], right_sem.at[at], down_device)

    to_core = remote(c_ref, near, near_sem.at[0], near_sem.at[1], core_device)
    mine_last = c_ref.at[last]
    to_detour = remote(mine_last, detour, send_sem.at[2], detour_sem.at[0], up_device)
    to_skip = remote(mine_last, detour, send_sem.at[1], detour_sem.at[0], skip_device)
    from_detour = remote(
        detour, left.at[last], detour_sem.at[1], left_sem.at[SIDES - 1], inner_device
    )
    from_skip = remote(
        detour, far.at[last], detour_sem.at[1], far_sem.at[len(FAR) - 1], skipped_device
    )

    def each(body, chunks):
        @pl.loop(0, EVEN)
        def _(k):
            body(k)

        for k in range(EVEN, chunks):
            body(k)

    def side_rows(p):
        return pl.ds(pl.multiple_of(p * TAIL, TAIL), TAIL)

    barrier = pltpu.get_barrier_semaphore()

    def greet(*devices):
        for device in devices:
            pl.semaphore_signal(barrier, inc=1, device_id=device, device_id_type=MESH)

    greet(core_device)
    pl.when(wrap)(lambda: greet(inner_device, outer_device))
    pl.when(jnp.logical_not(wrap))(lambda: greet(far_device))
    pl.when(even)(lambda: greet(up_device, down_device))
    pl.when(high_wrap)(lambda: greet(skip_device, skipped_device, skipping_device))

    for load in loads:
        load.start()

    pl.semaphore_wait(barrier, jnp.where(wrap, 3, 2) + jnp.where(even, 0, 2) + jnp.where(high_wrap, 3, 0))

    @pl.when(jnp.logical_not(even))
    def _():
        for device in (up_device, down_device):
            pl.semaphore_signal(ready_sem, inc=1, device_id=device, device_id_type=MESH)

    @pl.when(high_wrap)
    def _():
        to_detour.start()

    @pl.when(wrap)
    def _():
        each(lambda k: to_inner(chunk(k), k).start(), DETOUR)

    @pl.when(low_wrap)
    def _():
        for k in range(DETOUR, CHUNKS):
            to_inner(chunk(k), k).start()

    @pl.when(jnp.logical_not(wrap))
    def _():
        for at, rows in enumerate(FAR):
            to_far(pl.ds(*rows), at).start()

    @pl.when(high_wrap)
    def _():
        to_skip.start()

    @pl.when(even)
    def _():
        pl.semaphore_wait(ready_sem, 2)

    @pl.when(jnp.logical_not(low_wrap))
    def _():
        @pl.loop(0, SIDES)
        def _(p):
            to_down(side_rows(p), p).start()

    @pl.when(jnp.logical_not(high_wrap))
    def _():
        @pl.loop(0, SIDES)
        def _(p):
            to_up(side_rows(p), p).start()

    def forward(k):
        rows = chunk(k)
        rest = isinstance(k, int) and k >= EVEN
        side_at, far_block = (SIDES - 1, len(FAR) - 1) if rest else (k // 2, k // 4)

        @pl.when(wrap)
        def _():
            to_inner(rows, k).wait_recv()

        @pl.when(high_wrap)
        def _():
            to_up(rows, side_at, relay).start()

        @pl.when(low_wrap)
        def _():
            to_down(rows, side_at, relay).start()

        @pl.when(wrap)
        def _():
            to_outer = to_far(rows, far_block, relay, outer_device)
            to_outer.start()

    near_at = jnp.where(core == 1, 0, 2 * S)
    far_at = 2 * S - near_at
    mine = pl.ds(S, S)

    def third(i):
        return pl.ds(pl.multiple_of(i * 256, 256), 256)

    def select(blocks, links, counts, t, group, rows):
        total = None
        for l in range(LIST):
            used = jnp.logical_and(links[t, l] == group, l < counts[t])
            term = jnp.where(used, 1.0, 0.0) * blocks[t, l, rows, :]
            total = term if total is None else total + term
        return total

    def build(s):
        for t in range(GPD):
            beta_group = lax.rem(GPD * (b + nb - 1) + s, GPD * nb)
            alpha_group = lax.rem(GPD * (a + na - 1) + s, GPD * na)
            at = pl.multiple_of(s * G, 128)

            @pl.loop(0, G // 64)
            def _(i):
                rows = pl.ds(pl.multiple_of(i * 64, 64), 64)
                high, low = split(select(hb, lb_ref, cb_ref, t, beta_group, rows))
                to = (pl.ds(pl.multiple_of(at + i * 64, 64), 64), pl.ds(t * G, G))
                kb_h[to], kb_l[to] = high, low
                high, low = split(select(ha, la_ref, ca_ref, t, alpha_group, rows))
                to = (pl.ds(pl.multiple_of(t * G + i * 64, 64), 64), pl.ds(at, G))
                ka_h[to], ka_l[to] = high, low

        rows = pl.ds(pl.multiple_of(s * 128, 128), 128)
        own_h[rows, :], own_l[rows, :] = split(own[rows, :])

    def side(copy, block, at, p):
        rows, theirs = side_rows(p), pl.ds(at, S)
        copy(rows, p).wait_recv()
        out_ref[rows, :] += product(*split(block[rows, :]), kb_h[theirs, :], kb_l[theirs, :])

    def sides(p):
        side(to_down, right, 2 * S, p)
        side(to_up, left, 0, p)

    def stack(at):
        first, size = FAR[at]
        to_far(pl.ds(first, size), at).wait_recv()
        high, low = split(far[pl.ds(first, size), :])
        return jnp.concatenate([high, high, low], axis=0)

    def widen(block, first, size):
        theirs = pl.ds(pl.multiple_of(far_at + first, 128), size)
        high, low = ka_h[block, theirs], ka_l[block, theirs]
        return jnp.concatenate([high, low, high], axis=1)

    def outer(at):
        first, size = FAR[at]
        stacked = stack(at)

        @pl.loop(0, 3)
        def _(i):
            block = third(i)
            wide = widen(block, first, size)
            out_ref[block, :] += jnp.dot(wide, stacked, preferred_element_type=jnp.float32)

    for load in loads:
        load.wait()

    @pl.loop(0, 2)
    def _(step):
        forward(step)

        @pl.loop(0, 3)
        def _(i):
            build(3 * step + i)

    forward(2)
    to_core.start()

    @pl.loop(0, 3)
    def _(i):
        rows = third(i)
        out_ref[rows, :] = product(own_h[rows, :], own_l[rows, :], kb_h[mine, :], kb_l[mine, :])

    forward(3)

    @pl.loop(0, 3)
    def _(i):
        rows = third(i)
        out_ref[rows, :] += product(ka_h[rows, mine], ka_l[rows, mine], own_h[...], own_l[...])

    forward(4)
    to_core.wait_recv()

    @pl.when(low_wrap)
    def _():
        to_detour.wait_recv()
        from_detour.start()

    @pl.when(high_wrap)
    def _():
        to_skip.wait_recv()
        from_skip.start()

    @pl.loop(0, 3)
    def _(i):
        rows = third(i)
        near_h[rows, :], near_l[rows, :] = split(near[rows, :])
        wide_ref[rows, :] = widen(rows, S - TAIL, TAIL)

    forward(5)

    @pl.loop(0, 3)
    def _(i):
        rows = third(i)
        theirs = pl.ds(pl.multiple_of(near_at, 256), S)
        out_ref[rows, :] += product(ka_h[rows, theirs], ka_l[rows, theirs], near_h[...], near_l[...])

    forward(6)
    sides(0)
    forward(7)
    sides(1)
    forward(8)
    outer(0)
    forward(9)
    sides(2)
    forward(EVEN)
    outer(1)

    @pl.when(low_wrap)
    def _():
        forward(DETOUR)

    sides(3)

    @pl.when(low_wrap)
    def _():
        forward(DETOUR + 1)

    sides(4)
    outer(2)
    to_core.wait_send()
    sides(SIDES - 1)
    stacked_ref[...] = stack(len(FAR) - 1)

    @pl.when(high_wrap)
    def _():
        to_inner(most, 0).wait_send()

    @pl.when(low_wrap)
    def _():
        to_inner(whole, 0).wait_send()

    @pl.when(wrap)
    def _():
        from_detour.wait_send()

    to_far(whole, 0).wait_send()
    to_up(whole, 0).wait_send()
    to_down(whole, 0).wait_send()


def store(total_ref, wide_ref, stacked_ref, out_ref, result, sem):
    size = S // STORES
    copies = []
    for i in range(STORES):
        rows = pl.ds(i * size, size)
        result[rows, :] = total_ref[rows, :] + jnp.dot(
            wide_ref[rows, :], stacked_ref[...], preferred_element_type=jnp.float32
        )
        copies.append(pltpu.make_async_copy(result.at[rows], out_ref.at[rows], sem.at[i]))
        copies[-1].start()
    for copy in copies:
        copy.wait()


def solution(mesh):
    na, nb = mesh.shape["alpha"], mesh.shape["beta"]

    def on_device(
        coefficients, beta_blocks, alpha_blocks, beta_links, alpha_links, beta_count, alpha_count
    ):
        block = pltpu.VMEM((S, S), jnp.float32)
        listed = pltpu.VMEM((GPD, LIST, G, G), jnp.float32)
        half = pltpu.VMEM((S, S), jnp.bfloat16)
        tall = pltpu.VMEM((3 * S, S), jnp.bfloat16)
        wide = pltpu.VMEM((S, 3 * S), jnp.bfloat16)
        total, wide_rows, stacked = pl.pallas_call(
            functools.partial(kernel, na, nb),
            out_shape=(
                pltpu.VMEM((S, S), jnp.float32),
                pltpu.VMEM((S, 3 * TAIL), jnp.bfloat16),
                pltpu.VMEM((3 * TAIL, S), jnp.bfloat16),
            ),
            in_specs=[pl.BlockSpec(memory_space=pltpu.HBM)] * 7,
            out_specs=[pl.BlockSpec(memory_space=pltpu.VMEM)] * 3,
            scratch_shapes=[pltpu.SMEM((GPD, LIST), jnp.int32)] * 2
            + [pltpu.SMEM((GPD,), jnp.int32)] * 2
            + [block] * 6
            + [pltpu.VMEM((LAST, S), jnp.float32)]
            + [listed] * 2
            + [half] * 4
            + [tall, tall, wide, wide]
            + [
                pltpu.SemaphoreType.DMA((4,)),
                pltpu.SemaphoreType.DMA((CHUNKS,)),
                pltpu.SemaphoreType.DMA((len(FAR),)),
                pltpu.SemaphoreType.DMA((SIDES,)),
                pltpu.SemaphoreType.DMA((SIDES,)),
                pltpu.SemaphoreType.DMA((2,)),
                pltpu.SemaphoreType.DMA((2,)),
                pltpu.SemaphoreType.DMA((7,)),
                pltpu.SemaphoreType.REGULAR,
            ],
            compiler_params=pltpu.CompilerParams(
                collective_id=0, has_side_effects=True, vmem_limit_bytes=58 * 2**20
            ),
            name="sigma",
        )(
            coefficients, beta_blocks, alpha_blocks,
            beta_links, alpha_links, beta_count, alpha_count,
        )
        return pl.pallas_call(
            store,
            out_shape=jax.ShapeDtypeStruct((S, S), jnp.float32),
            in_specs=[pl.BlockSpec(memory_space=pltpu.VMEM)] * 3,
            out_specs=pl.BlockSpec(memory_space=pl.ANY),
            scratch_shapes=[block, pltpu.SemaphoreType.DMA((STORES,))],
            compiler_params=pltpu.CompilerParams(vmem_limit_bytes=8 * 2**20),
            name="store",
        )(total, wide_rows, stacked)

    return jax.shard_map(
        on_device,
        mesh=mesh,
        in_specs=(
            P("alpha", "beta"),
            P("beta", None, None, None),
            P("alpha", None, None, None),
            P("beta", None),
            P("alpha", None),
            P("beta"),
            P("alpha"),
        ),
        out_specs=P("alpha", "beta"),
        check_vma=False,
    )
```

```python
import functools

import jax
import jax.numpy as jnp
from jax import lax
from jax.experimental import pallas as pl
from jax.experimental.pallas import tpu as pltpu
from jax.sharding import PartitionSpec as P

MESH = pl.DeviceIdType.MESH
G = 384
GPD = 2
LIST = 3
S = G * GPD
R = 64
EVEN = 10
REST = ((640, 32), (672, 64), (736, 32))
CHUNKS = EVEN + len(REST)
DETOUR = EVEN + 1
LAST = S - REST[1][0]
FAR = ((0, 256), (256, 256), (512, 128), (640, 128))
STORES = 6
TAIL = 128
SIDES = S // TAIL


def split(x):
    high = x.astype(jnp.bfloat16)
    return high, (x - high.astype(jnp.float32)).astype(jnp.bfloat16)


def product(a_high, a_low, b_high, b_low):
    dot = functools.partial(jnp.dot, preferred_element_type=jnp.float32)
    return dot(a_high, b_high) + dot(a_low, b_high) + dot(a_high, b_low)


def chunk(k):
    if isinstance(k, int) and k >= EVEN:
        return pl.ds(*REST[k - EVEN])
    return pl.ds(k * R, R)


def kernel(
    na, nb,
    c_ref, hb_ref, ha_ref, lb_in, la_in, cb_in, ca_in,
    out_ref, wide_ref, stacked_ref,
    lb_ref, la_ref, cb_ref, ca_ref, own, near, far, left, right, relay, detour, hb, ha,
    own_h, own_l, near_h, near_l, kb_h, kb_l, ka_h, ka_l,
    send_sem, relay_sem, far_sem, left_sem, right_sem, near_sem, detour_sem, local_sem, ready_sem,
):
    a, b = lax.axis_index("alpha"), lax.axis_index("beta")
    nz = nb // 2
    core, z = lax.rem(a, 2), lax.rem(b, nz)

    def turned(a):
        return a + 2 - 4 * lax.rem(a // 2, 2)

    column = b - z
    low_wrap, high_wrap = z == 0, z == nz - 1
    wrap = jnp.logical_or(low_wrap, high_wrap)
    even = lax.rem(z, 2) == 0
    far_a, inner_b = lax.rem(a + 2 * core + na - 1, na), lax.rem(b + nz, nb)
    core_device = (a + 1 - 2 * core, b)
    inner_device = (a, inner_b)
    outer_device = (far_a, inner_b)
    far_device = (far_a, b)
    other_a = turned(a)
    skip_device = (other_a, inner_b)
    skipped_device = (lax.rem(other_a + 2 * core + na - 1, na), inner_b)
    skipping_device = (turned(far_a), inner_b)
    up_device = (a, column + lax.rem(z + 1, nz))
    down_device = (a, column + lax.rem(z + nz - 1, nz))

    loads = [
        pltpu.make_async_copy(source, target, local_sem.at[i])
        for i, (source, target) in enumerate(
            (
                (lb_in, lb_ref), (la_in, la_ref), (cb_in, cb_ref), (ca_in, ca_ref),
                (hb_ref, hb), (ha_ref, ha), (c_ref, own),
            )
        )
    ]

    whole, most, last = pl.ds(0, S), pl.ds(0, S - LAST), pl.ds(S - LAST, LAST)

    def remote(source, target, send, recv, device):
        return pltpu.make_async_remote_copy(
            src_ref=source, dst_ref=target, send_sem=send, recv_sem=recv,
            device_id=device, device_id_type=MESH,
        )

    def to_inner(rows, k):
        source, target = c_ref.at[rows], relay.at[rows]
        return remote(source, target, send_sem.at[0], relay_sem.at[k], inner_device)

    def to_far(rows, at, source=c_ref, device=far_device):
        return remote(source.at[rows], far.at[rows], send_sem.at[1], far_sem.at[at], device)

    def to_up(rows, at, source=c_ref):
        return remote(source.at[rows], left.at[rows], send_sem.at[2], left_sem.at[at], up_device)

    def to_down(rows, at, source=c_ref):
        source, target = source.at[rows], right.at[rows]
        return remote(source, target, send_sem.at[3], right_sem.at[at], down_device)

    to_core = remote(c_ref, near, near_sem.at[0], near_sem.at[1], core_device)
    mine_last = c_ref.at[last]
    to_detour = remote(mine_last, detour, send_sem.at[2], detour_sem.at[0], up_device)
    to_skip = remote(mine_last, detour, send_sem.at[1], detour_sem.at[0], skip_device)
    from_detour = remote(
        detour, left.at[last], detour_sem.at[1], left_sem.at[SIDES - 1], inner_device
    )
    from_skip = remote(
        detour, far.at[last], detour_sem.at[1], far_sem.at[len(FAR) - 1], skipped_device
    )

    def each(body, chunks):
        @pl.loop(0, EVEN)
        def _(k):
            body(k)

        for k in range(EVEN, chunks):
            body(k)

    def side_rows(p):
        return pl.ds(pl.multiple_of(p * TAIL, TAIL), TAIL)

    barrier = pltpu.get_barrier_semaphore()

    def greet(*devices):
        for device in devices:
            pl.semaphore_signal(barrier, inc=1, device_id=device, device_id_type=MESH)

    greet(core_device)
    pl.when(wrap)(lambda: greet(inner_device, outer_device))
    pl.when(jnp.logical_not(wrap))(lambda: greet(far_device))
    pl.when(even)(lambda: greet(up_device, down_device))
    pl.when(high_wrap)(lambda: greet(skip_device, skipped_device, skipping_device))

    for load in loads:
        load.start()

    pl.semaphore_wait(barrier, jnp.where(wrap, 3, 2) + jnp.where(even, 0, 2) + jnp.where(high_wrap, 3, 0))

    @pl.when(jnp.logical_not(even))
    def _():
        for device in (up_device, down_device):
            pl.semaphore_signal(ready_sem, inc=1, device_id=device, device_id_type=MESH)

    @pl.when(high_wrap)
    def _():
        to_detour.start()

    @pl.when(wrap)
    def _():
        each(lambda k: to_inner(chunk(k), k).start(), DETOUR)

    @pl.when(low_wrap)
    def _():
        for k in range(DETOUR, CHUNKS):
            to_inner(chunk(k), k).start()

    @pl.when(jnp.logical_not(wrap))
    def _():
        for at, rows in enumerate(FAR):
            to_far(pl.ds(*rows), at).start()

    @pl.when(high_wrap)
    def _():
        to_skip.start()

    @pl.when(even)
    def _():
        pl.semaphore_wait(ready_sem, 2)

    @pl.when(jnp.logical_not(low_wrap))
    def _():
        @pl.loop(0, SIDES)
        def _(p):
            to_down(side_rows(p), p).start()

    @pl.when(jnp.logical_not(high_wrap))
    def _():
        @pl.loop(0, SIDES)
        def _(p):
            to_up(side_rows(p), p).start()

    def forward(k):
        rows = chunk(k)
        rest = isinstance(k, int) and k >= EVEN
        side_at, far_block = (SIDES - 1, len(FAR) - 1) if rest else (k // 2, k // 4)

        @pl.when(wrap)
        def _():
            to_inner(rows, k).wait_recv()

        @pl.when(high_wrap)
        def _():
            to_up(rows, side_at, relay).start()

        @pl.when(low_wrap)
        def _():
            to_down(rows, side_at, relay).start()

        @pl.when(wrap)
        def _():
            to_outer = to_far(rows, far_block, relay, outer_device)
            to_outer.start()

    near_at = jnp.where(core == 1, 0, 2 * S)
    far_at = 2 * S - near_at
    mine = pl.ds(S, S)

    def third(i):
        return pl.ds(pl.multiple_of(i * 256, 256), 256)

    def select(blocks, links, counts, t, group, rows):
        total = None
        for l in range(LIST):
            used = jnp.logical_and(links[t, l] == group, l < counts[t])
            term = jnp.where(used, 1.0, 0.0) * blocks[t, l, rows, :]
            total = term if total is None else total + term
        return total

    def build(s):
        for t in range(GPD):
            beta_group = lax.rem(GPD * (b + nb - 1) + s, GPD * nb)
            alpha_group = lax.rem(GPD * (a + na - 1) + s, GPD * na)
            at = pl.multiple_of(s * G, 128)

            @pl.loop(0, G // 64)
            def _(i):
                rows = pl.ds(pl.multiple_of(i * 64, 64), 64)
                high, low = split(select(hb, lb_ref, cb_ref, t, beta_group, rows))
                to = (pl.ds(pl.multiple_of(at + i * 64, 64), 64), pl.ds(t * G, G))
                kb_h[to], kb_l[to] = high, low
                high, low = split(select(ha, la_ref, ca_ref, t, alpha_group, rows))
                to = (pl.ds(pl.multiple_of(t * G + i * 64, 64), 64), pl.ds(at, G))
                ka_h[to], ka_l[to] = high, low

        rows = pl.ds(pl.multiple_of(s * 128, 128), 128)
        own_h[rows, :], own_l[rows, :] = split(own[rows, :])

    def side(copy, block, at, p):
        rows, theirs = side_rows(p), pl.ds(at, S)
        copy(rows, p).wait_recv()
        out_ref[rows, :] += product(*split(block[rows, :]), kb_h[theirs, :], kb_l[theirs, :])

    def sides(p):
        side(to_down, right, 2 * S, p)
        side(to_up, left, 0, p)

    def stack(at):
        first, size = FAR[at]
        to_far(pl.ds(first, size), at).wait_recv()
        high, low = split(far[pl.ds(first, size), :])
        return jnp.concatenate([high, high, low], axis=0)

    def widen(block, first, size):
        theirs = pl.ds(pl.multiple_of(far_at + first, 128), size)
        high, low = ka_h[block, theirs], ka_l[block, theirs]
        return jnp.concatenate([high, low, high], axis=1)

    def outer(at):
        first, size = FAR[at]
        stacked = stack(at)

        @pl.loop(0, 3)
        def _(i):
            block = third(i)
            wide = widen(block, first, size)
            out_ref[block, :] += jnp.dot(wide, stacked, preferred_element_type=jnp.float32)

    for load in loads:
        load.wait()

    @pl.loop(0, 2)
    def _(step):
        forward(step)

        @pl.loop(0, 3)
        def _(i):
            build(3 * step + i)

    forward(2)
    to_core.start()

    @pl.loop(0, 3)
    def _(i):
        rows = third(i)
        out_ref[rows, :] = product(own_h[rows, :], own_l[rows, :], kb_h[mine, :], kb_l[mine, :])

    forward(3)

    @pl.loop(0, 3)
    def _(i):
        rows = third(i)
        out_ref[rows, :] += product(ka_h[rows, mine], ka_l[rows, mine], own_h[...], own_l[...])

    forward(4)
    to_core.wait_recv()

    @pl.when(low_wrap)
    def _():
        to_detour.wait_recv()
        from_detour.start()

    @pl.when(high_wrap)
    def _():
        to_skip.wait_recv()
        from_skip.start()

    @pl.loop(0, 3)
    def _(i):
        rows = third(i)
        near_h[rows, :], near_l[rows, :] = split(near[rows, :])
        wide_ref[rows, :] = widen(rows, S - TAIL, TAIL)

    forward(5)

    @pl.loop(0, 3)
    def _(i):
        rows = third(i)
        theirs = pl.ds(pl.multiple_of(near_at, 256), S)
        out_ref[rows, :] += product(ka_h[rows, theirs], ka_l[rows, theirs], near_h[...], near_l[...])

    forward(6)
    sides(0)
    forward(7)
    sides(1)
    forward(8)
    outer(0)
    forward(9)
    sides(2)
    forward(EVEN)
    outer(1)

    @pl.when(low_wrap)
    def _():
        forward(DETOUR)

    sides(3)

    @pl.when(low_wrap)
    def _():
        forward(DETOUR + 1)

    sides(4)
    outer(2)
    to_core.wait_send()
    sides(SIDES - 1)
    stacked_ref[...] = stack(len(FAR) - 1)

    @pl.when(high_wrap)
    def _():
        to_inner(most, 0).wait_send()

    @pl.when(low_wrap)
    def _():
        to_inner(whole, 0).wait_send()

    @pl.when(wrap)
    def _():
        from_detour.wait_send()

    to_far(whole, 0).wait_send()
    to_up(whole, 0).wait_send()
    to_down(whole, 0).wait_send()


def store(total_ref, wide_ref, stacked_ref, out_ref, result, sem):
    size = S // STORES
    copies = []
    for i in range(STORES):
        rows = pl.ds(i * size, size)
        result[rows, :] = total_ref[rows, :] + jnp.dot(
            wide_ref[rows, :], stacked_ref[...], preferred_element_type=jnp.float32
        )
        copies.append(pltpu.make_async_copy(result.at[rows], out_ref.at[rows], sem.at[i]))
        copies[-1].start()
    for copy in copies:
        copy.wait()


def solution(mesh):
    na, nb = mesh.shape["alpha"], mesh.shape["beta"]

    def on_device(
        coefficients, beta_blocks, alpha_blocks, beta_links, alpha_links, beta_count, alpha_count
    ):
        block = pltpu.VMEM((S, S), jnp.float32)
        listed = pltpu.VMEM((GPD, LIST, G, G), jnp.float32)
        half = pltpu.VMEM((S, S), jnp.bfloat16)
        tall = pltpu.VMEM((3 * S, S), jnp.bfloat16)
        wide = pltpu.VMEM((S, 3 * S), jnp.bfloat16)
        total, wide_rows, stacked = pl.pallas_call(
            functools.partial(kernel, na, nb),
            out_shape=(
                pltpu.VMEM((S, S), jnp.float32),
                pltpu.VMEM((S, 3 * TAIL), jnp.bfloat16),
                pltpu.VMEM((3 * TAIL, S), jnp.bfloat16),
            ),
            in_specs=[pl.BlockSpec(memory_space=pltpu.HBM)] * 7,
            out_specs=[pl.BlockSpec(memory_space=pltpu.VMEM)] * 3,
            scratch_shapes=[pltpu.SMEM((GPD, LIST), jnp.int32)] * 2
            + [pltpu.SMEM((GPD,), jnp.int32)] * 2
            + [block] * 6
            + [pltpu.VMEM((LAST, S), jnp.float32)]
            + [listed] * 2
            + [half] * 4
            + [tall, tall, wide, wide]
            + [
                pltpu.SemaphoreType.DMA((4,)),
                pltpu.SemaphoreType.DMA((CHUNKS,)),
                pltpu.SemaphoreType.DMA((len(FAR),)),
                pltpu.SemaphoreType.DMA((SIDES,)),
                pltpu.SemaphoreType.DMA((SIDES,)),
                pltpu.SemaphoreType.DMA((2,)),
                pltpu.SemaphoreType.DMA((2,)),
                pltpu.SemaphoreType.DMA((7,)),
                pltpu.SemaphoreType.REGULAR,
            ],
            compiler_params=pltpu.CompilerParams(
                collective_id=0, has_side_effects=True, vmem_limit_bytes=58 * 2**20
            ),
            name="sigma",
        )(
            coefficients, beta_blocks, alpha_blocks,
            beta_links, alpha_links, beta_count, alpha_count,
        )
        return pl.pallas_call(
            store,
            out_shape=jax.ShapeDtypeStruct((S, S), jnp.float32),
            in_specs=[pl.BlockSpec(memory_space=pltpu.VMEM)] * 3,
            out_specs=pl.BlockSpec(memory_space=pl.ANY),
            scratch_shapes=[block, pltpu.SemaphoreType.DMA((STORES,))],
            compiler_params=pltpu.CompilerParams(vmem_limit_bytes=8 * 2**20),
            name="store",
        )(total, wide_rows, stacked)

    return jax.shard_map(
        on_device,
        mesh=mesh,
        in_specs=(
            P("alpha", "beta"),
            P("beta", None, None, None),
            P("alpha", None, None, None),
            P("beta", None),
            P("alpha", None),
            P("beta"),
            P("alpha"),
        ),
        out_specs=P("alpha", "beta"),
        check_vma=False,
    )
```
